256 devices in a mesh: ctx: 32 (over x, y, core), ch: 8 (over z).
Axes of the slice: x: 4, y: 4, z: 8, core: 2. Of those that a mesh axis runs over, the one named last changes fastest.
Arguments:
- gate_input: bfloat16 [8192, 16384], P('ch', 'ctx'), may hold values from -90 to 90
- key_input: bfloat16 [8192, 16384], P('ch', 'ctx'), may hold values from -6 to 6
- value_input: bfloat16 [8192, 16384], P('ch', 'ctx'), may hold values from -6 to 6
- short_filter: float32 [3, 3, 8192], P(None, None, 'ch'), may hold values from -3.5 to 3.5
- mr_filter: float32 [512, 128], P('ch'), may hold values from -0.5 to 0.5
- mr_skip: float32 [8192], P('ch'), may hold values from -3 to 3
- norm_gain: float32 [8192], P('ch'), may hold values from 0.5 to 1.5
- doc_lengths: int32 [64], replicated, may hold values from 1 to 2048, 16384 in all
Outputs:
- relaid: bfloat16 [8192, 16384], P(('ch', 'ctx'))
The draws below stay inside these ranges and needn't reach their ends.
Inputs may be any that keep to these rules, and one draw needn't show every extreme that they name: `doc_lengths`: the 64 lengths sum to 16384, and one of them is exactly 2048.
All inputs are finite; a program needn't handle non-finite values.
Results may differ from the reference program's by a relative error of at most 0.0095.
Values may be sent and summed in bfloat16 or wider, within the bound.
No kernel may reach another device: no remote copies, remote signals or barrier semaphores. Data moves between devices by JAX's collectives and lax.ppermute only.
A program may use at most 128 MiB of HBM per device.

```python
import math
import jax
import jax.numpy as jnp
import numpy as np
from jax import lax

D = 8192
GROUP = 16
GROUPS = 512
SHORT = 3
MR = 128
TOKENS = 16384
DOCS = 64
DOC_MOST = 2048


def draw_gate_input(key, part):
    noise_key, chan_key, row_key = jax.random.split(key, 3)
    chan_place = jnp.arange(D, dtype=jnp.float32) / D
    chan_scale = jnp.exp(jax.random.uniform(chan_key, (D, 1), jnp.float32) * math.log(10.0)) * jnp.sqrt(1.0 + 2.0 * chan_place)[:, None]
    row_scale = jnp.exp(jax.random.uniform(row_key, (1, TOKENS), jnp.float32) * math.log(10.0))
    base_values = jnp.clip(jax.random.normal(noise_key, (D, TOKENS), jnp.float32), -5.0, 5.0)
    return (base_values * chan_scale * row_scale / 10.0).astype(jnp.bfloat16)


def steps_of(rng, dims, shards, low, largest):
    def one(axis_at, parts):
        heights = jax.random.uniform(jax.random.fold_in(jax.random.fold_in(rng, 6), axis_at), (parts,), jnp.float32, low / len(shards), largest / len(shards))
        return jnp.repeat(jnp.exp(heights), dims[axis_at] // parts).reshape((-1,) + (1,) * (len(dims) - axis_at - 1))

    factor_of = one(*shards[0])
    for cut in shards[1:]:
        factor_of = factor_of * one(*cut)
    return factor_of


def length_profile(number_of, total, limit, slope):
    weights = [(1 << 20) // math.isqrt(standing ** slope) + 1 for standing in range(2, number_of + 1)]
    rest, counts = total - limit - (number_of - 1), [1] * (number_of - 1)
    while rest > 0:
        candidates = [i for i in range(number_of - 1) if counts[i] < limit]
        pool, left = sum([weights[i] for i in candidates]), rest
        for i in candidates:
            addition = min(limit - counts[i], max(1, left * weights[i] // pool), rest)
            counts[i] = counts[i] + addition
            rest = rest - addition
    return np.array([limit] + counts)


def ragged_sizes(key, amount, total, reach, skew):
    if amount == 2:
        one = jax.random.randint(key, (), max(1, total - reach), min(reach, total - 1) + 1)
        return jnp.stack([one, total - one])
    tallies = jnp.asarray(length_profile(amount, total, reach, skew), jnp.int32)
    twos = (amount - 1) // 2
    donor, receiver = tallies[1:1 + 2 * twos:2], tallies[2:2 + 2 * twos:2]
    margin = jnp.minimum(donor - 1, reach - receiver)
    moved = jax.random.randint(jax.random.fold_in(key, 1), (twos,), 0, 1 << 20) % (margin + 1)
    tallies = tallies.at[1:1 + 2 * twos:2].set(donor - moved).at[2:2 + 2 * twos:2].set(receiver + moved)
    return tallies[jax.random.permutation(jax.random.fold_in(key, 2), amount)]


def bell_draw(own_key, dims, width, most, shards=(), held_as=jnp.bfloat16):
    loudness = steps_of(own_key, dims, shards, -0.22, 0.18) if shards else 1.0
    drawn = jax.random.normal(own_key, dims, jnp.float32) * width * loudness
    return jnp.minimum(jnp.maximum(drawn, -most), most).astype(held_as)


def setup_inputs(seed: int = 0) -> dict:
    keys = jax.random.split(jax.random.key(seed), 9)
    gate_input = draw_gate_input(jax.random.fold_in(keys[8], 71), 0)
    key_input = bell_draw(keys[1], (D, TOKENS), 1.0, 6.0, ((0, 8), (1, 32)))
    value_input = bell_draw(keys[2], (D, TOKENS), 1.0, 6.0, ((0, 8), (1, 32)))
    short_filter = bell_draw(keys[3], (3, SHORT, D), SHORT ** -0.5, 3.5, ((2, 8),), jnp.float32)
    mr_filter = bell_draw(keys[4], (GROUPS, MR), MR ** -0.5, 0.5, ((0, 8),), jnp.float32)
    mr_skip = bell_draw(keys[5], (D,), 1.0, 3.0, ((0, 8),), jnp.float32)
    norm_gain = jnp.clip(1.0 + 0.1 * jax.random.normal(keys[6], (D,), jnp.float32), 0.5, 1.5)
    doc_lengths = ragged_sizes(keys[7], DOCS, TOKENS, DOC_MOST, 2).astype(jnp.int32)
    return dict(gate_input=gate_input, key_input=key_input, value_input=value_input, short_filter=short_filter, mr_filter=mr_filter, mr_skip=mr_skip, norm_gain=norm_gain, doc_lengths=doc_lengths)


NORM_EPS = 1e-06

def doc_starts(doc_lengths, positions):
    doc_ends = jnp.cumsum(doc_lengths).astype(jnp.int32)
    doc_firsts = (doc_ends - doc_lengths).astype(jnp.int32)
    before_row = doc_firsts[:, None] <= positions[None, :]
    return lax.optimization_barrier(jnp.max(jnp.where(before_row, doc_firsts[:, None], 0), axis=0)).astype(jnp.int32)

def short_conv(raw_rows, prior_rows, tap_rows, positions, starts):
    row_count = raw_rows.shape[1]
    extended = jnp.concatenate([prior_rows, raw_rows], axis=1).astype(jnp.float32)
    running = jnp.zeros(raw_rows.shape, jnp.float32)
    for tap_lag in range(SHORT):
        lagged = lax.slice_in_dim(extended, SHORT - 1 - tap_lag, SHORT - 1 - tap_lag + row_count, axis=1)
        in_document = positions - tap_lag >= starts
        running = running + jnp.where(in_document[None, :], tap_rows[tap_lag][:, None] * lagged, 0.0)
    return running

def toeplitz(taps_bf):
    row_index = np.arange(2 * MR)[:, None]
    col_index = np.arange(MR)[None, :]
    tap_lag = col_index + MR - row_index
    is_valid = (tap_lag >= 0) & (tap_lag < MR)
    index_table = np.clip(tap_lag, 0, MR - 1)
    return jnp.where(is_valid[None], taps_bf[:, index_table], jnp.zeros((), jnp.bfloat16))

def long_conv(values, prior_rows, taps_bf, first_row, starts):
    channels, row_count = values.shape
    groups = taps_bf.shape[0]
    members = channels // groups
    tile_count = row_count // MR
    blocked = jnp.concatenate([prior_rows, values], axis=1).reshape(channels, tile_count + 1, MR)
    windows = jnp.concatenate([blocked[:, :-1], blocked[:, 1:]], axis=2).reshape(groups, members, tile_count, 2 * MR)
    matrices = toeplitz(taps_bf)
    per_step = math.gcd(tile_count, max(1, 64 // groups))
    tile_starts = starts.reshape(tile_count, MR)
    source_offsets = jnp.arange(2 * MR, dtype=jnp.int32) - MR
    step_offsets = jnp.arange(per_step, dtype=jnp.int32) * MR
    zero_bf = jnp.zeros((), jnp.bfloat16)

    def advance(step_index, result):
        block_begin = step_index * per_step
        window_part = lax.dynamic_slice_in_dim(windows, block_begin, per_step, axis=2)
        row_starts = lax.dynamic_slice_in_dim(tile_starts, block_begin, per_step, axis=0)
        tile_first = first_row + block_begin * MR + step_offsets
        sources = tile_first[:, None] + source_offsets[None, :]
        allowed = sources[:, :, None] >= row_starts[:, None, :]
        masked = jnp.where(allowed[:, None], matrices[None], zero_bf)
        product = jnp.einsum('gcns,ngst->gcnt', window_part.astype(jnp.float32), masked.astype(jnp.float32))
        return lax.dynamic_update_slice_in_dim(result, product, block_begin, axis=2)
    result = lax.fori_loop(0, tile_count // per_step, advance, jnp.zeros((groups, members, tile_count, MR), jnp.float32))
    return result.reshape(channels, row_count)

def reference(gate_input, key_input, value_input, short_filter, mr_filter, mr_skip, norm_gain, doc_lengths):
    positions = jnp.arange(TOKENS, dtype=jnp.int32)
    starts = doc_starts(doc_lengths, positions)
    chan_block = min(D, 1024)
    zero_prior = jnp.zeros((chan_block, SHORT - 1), jnp.bfloat16)
    zero_rows = jnp.zeros((chan_block, MR), jnp.bfloat16)
    squares = jnp.zeros((TOKENS,), jnp.float32)
    pieces = []
    for block_index in range(D // chan_block):
        chan_first = block_index * chan_block
        chan_last = chan_first + chan_block
        gate_conv = short_conv(gate_input[chan_first:chan_last], zero_prior, short_filter[0, :, chan_first:chan_last], positions, starts)
        key_conv = short_conv(key_input[chan_first:chan_last], zero_prior, short_filter[1, :, chan_first:chan_last], positions, starts)
        value_conv = short_conv(value_input[chan_first:chan_last], zero_prior, short_filter[2, :, chan_first:chan_last], positions, starts)
        product_rows = (key_conv * value_conv).astype(jnp.bfloat16)
        taps_bf = mr_filter[chan_first // GROUP:chan_last // GROUP].astype(jnp.bfloat16)
        mixed_rows = long_conv(product_rows, zero_rows, taps_bf, 0, starts) + mr_skip[chan_first:chan_last, None] * product_rows.astype(jnp.float32)
        gated = gate_conv * mixed_rows
        squares = squares + lax.optimization_barrier(jnp.sum(gated * gated, axis=0))
        pieces.append(gated)
    row_scale = lax.rsqrt(squares / D + NORM_EPS)
    results = []
    for block_index in range(D // chan_block):
        chan_first = block_index * chan_block
        gain_part = norm_gain[chan_first:chan_first + chan_block]
        results.append((pieces[block_index] * row_scale[None, :] * gain_part[:, None]).astype(jnp.bfloat16))
    return jnp.concatenate(results, axis=0)
```

```python
import functools
import math
import jax
import jax.numpy as jnp
from jax import lax
from jax.experimental import pallas as pl
from jax.experimental.pallas import tpu as pltpu
from jax.sharding import PartitionSpec as P

D = 8192
GROUP = 16
MR = 128
EPS = 1e-6
DOCS = 64
F32 = jnp.float32
BF = jnp.bfloat16
CB = 128


def starts_row(docs_ref, base, count):
    pos = lax.broadcasted_iota(jnp.int32, (1, count), 1) + base
    first = jnp.int32(0)
    start = jnp.zeros((1, count), jnp.int32)
    for d in range(DOCS):
        start = jnp.where(pos >= first, first, start)
        first = first + docs_ref[d]
    return pos, start


def columns(sf_ref, skip_ref, gain_ref):
    rows = [sf_ref[0], sf_ref[1], sf_ref[2], skip_ref[...], gain_ref[...],
            jnp.zeros((5, CB), F32)]
    return jnp.concatenate(rows, axis=0).T


def conv3(cur, prev, cols, first, keep1, keep2):
    w = cur.shape[1]
    ext = jnp.concatenate([prev, cur], axis=1)
    one = pltpu.roll(ext, 1, 1)[:, 128:]
    two = pltpu.roll(ext, 2, 1)[:, 128:]
    t0 = cols[:, first:first + 1]
    t1 = cols[:, first + 1:first + 2]
    t2 = cols[:, first + 2:first + 3]
    return t0 * cur + jnp.where(keep1, t1 * one, 0.0) + jnp.where(keep2, t2 * two, 0.0)


def tail_kernel(docs_ref, base_ref, gate_ref, key_ref, value_ref, sf_ref, skip_ref, gain_ref, out_ref):
    base = base_ref[0] + 384
    pos, start = starts_row(docs_ref, base, 128)
    keep1 = jnp.broadcast_to(pos - 1 >= start, (CB, 128))
    keep2 = jnp.broadcast_to(pos - 2 >= start, (CB, 128))
    cols = columns(sf_ref, skip_ref, gain_ref)
    key = key_ref[...].astype(F32)
    value = value_ref[...].astype(F32)
    gate = gate_ref[...].astype(F32)
    kc = conv3(key[:, 128:], key[:, :128], cols, 3, keep1, keep2)
    vc = conv3(value[:, 128:], value[:, :128], cols, 6, keep1, keep2)
    out_ref[:, :128] = (kc * vc).astype(BF)
    lane = lax.broadcasted_iota(jnp.int32, (CB, 128), 1)
    packed = jnp.where(lane >= 126, gate[:, 128:],
                       jnp.where(lane >= 124, pltpu.roll(key[:, 128:], 126, 1),
                                 pltpu.roll(value[:, 128:], 124, 1)))
    out_ref[:, 128:] = packed.astype(BF)


def main_kernel(docs_ref, base_ref, gate_ref, key_ref, value_ref, halo_ref, sf_ref, skip_ref,
                gain_ref, taps_ref, out_ref, sq_ref, masks, prod, mixed):
    n = gate_ref.shape[1]
    tiles = n // 128
    base = base_ref[0]
    pos, start = starts_row(docs_ref, base, n)

    @pl.when(pl.program_id(0) == 0)
    def _():
        s = lax.broadcasted_iota(jnp.int32, (128, 128), 0)
        t = lax.broadcasted_iota(jnp.int32, (128, 128), 1)
        for j in range(tiles):
            first = jnp.broadcast_to(start[:, 128 * j:128 * (j + 1)] - (base + 128 * j), (128, 128))
            prev = (s > t) & (s - 128 >= first)
            here = (s <= t) & (s >= first)
            masks[j, :128, :] = prev.astype(F32).astype(BF)
            masks[j, 128:, :] = here.astype(F32).astype(BF)
        sq_ref[...] = jnp.zeros_like(sq_ref)

    keep1 = jnp.broadcast_to(pos - 1 >= start, (CB, n))
    keep2 = jnp.broadcast_to(pos - 2 >= start, (CB, n))
    cols = columns(sf_ref, skip_ref, gain_ref)
    packed = halo_ref[:, 128:].astype(F32)
    kc = conv3(key_ref[...].astype(F32), pltpu.roll(packed, 2, 1), cols, 3, keep1, keep2)
    vc = conv3(value_ref[...].astype(F32), pltpu.roll(packed, 4, 1), cols, 6, keep1, keep2)
    prod[:, :128] = halo_ref[:, :128]
    prod[:, 128:] = (kc * vc).astype(BF)

    taps = taps_ref[...].astype(BF).astype(F32)
    for g in range(CB // GROUP):
        ring = pltpu.roll(jnp.broadcast_to(taps[g:g + 1], (128, 128)), 0, 1, stride=1, stride_axis=0).astype(BF)
        both = jnp.concatenate([ring, ring], axis=0)
        for j in range(tiles):
            mixed[GROUP * g:GROUP * (g + 1), 128 * j:128 * (j + 1)] = jnp.dot(
                prod[GROUP * g:GROUP * (g + 1), 128 * j:128 * j + 256], both * masks[j],
                preferred_element_type=F32)

    gc = conv3(gate_ref[...].astype(F32), packed, cols, 0, keep1, keep2)
    gated = gc * (mixed[...] + cols[:, 9:10] * prod[:, 128:].astype(F32))
    sq = gated * gated
    acc = sq[:8]
    for i in range(1, CB // 8):
        acc = acc + sq[8 * i:8 * i + 8]
    sq_ref[...] += acc
    out_ref[...] = (gated * cols[:, 10:11]).astype(BF)


def param_specs():
    return [
        pl.BlockSpec((3, 3, CB), lambda i: (0, 0, i)),
        pl.BlockSpec((1, CB), lambda i: (0, i)),
        pl.BlockSpec((1, CB), lambda i: (0, i)),
    ]

SMEM = pl.BlockSpec(memory_space=pltpu.SMEM)

def tail(docs, base, gate, key, value, sf, skip, gain):
    ch, n = gate.shape
    wide = pl.BlockSpec((CB, 256), lambda i: (i, n // 256 - 1))
    return pl.pallas_call(
        tail_kernel, grid=(ch // CB,),
        in_specs=[SMEM, SMEM, wide, wide, wide] + param_specs(),
        out_specs=pl.BlockSpec((CB, 256), lambda i: (i, 0)),
        out_shape=jax.ShapeDtypeStruct((ch, 256), BF), name="tail",
    )(docs, base, gate, key, value, sf, skip, gain)


def main(docs, base, gate, key, value, halo, sf, skip, gain, taps):
    ch, n = gate.shape
    wide = pl.BlockSpec((CB, n), lambda i: (i, 0))
    return pl.pallas_call(
        main_kernel, grid=(ch // CB,),
        in_specs=[SMEM, SMEM, wide, wide, wide, pl.BlockSpec((CB, 256), lambda i: (i, 0))] + param_specs()
        + [pl.BlockSpec((CB // GROUP, MR), lambda i: (i, 0))],
        out_specs=[wide, pl.BlockSpec((8, n), lambda i: (0, 0))],
        out_shape=[jax.ShapeDtypeStruct((ch, n), BF), jax.ShapeDtypeStruct((8, n), F32)],
        scratch_shapes=[pltpu.VMEM((n // 128, 256, 128), BF), pltpu.VMEM((CB, n + 128), BF), pltpu.VMEM((CB, n), F32)],
        compiler_params=pltpu.CompilerParams(vmem_limit_bytes=48 << 20), name="mixer",
    )(docs, base, gate, key, value, halo, sf, skip, gain, taps)


def final_kernel(recv_ref, sums_ref, out_ref):
    per = recv_ref.shape[0]
    n = recv_ref.shape[2]
    for i in range(per):
        scale = lax.rsqrt(sums_ref[i] / D + EPS)
        out_ref[:, n * i:n * (i + 1)] = (recv_ref[i].astype(F32) * scale).astype(BF)


def final(recv, sums, per=8):
    k, c, n = recv.shape
    return pl.pallas_call(
        final_kernel, grid=(k // per,),
        in_specs=[pl.BlockSpec((per, c, n), lambda i: (i, 0, 0)), pl.BlockSpec((per, 1, n), lambda i: (i, 0, 0))],
        out_specs=pl.BlockSpec((c, per * n), lambda i: (0, i)),
        out_shape=jax.ShapeDtypeStruct((c, k * n), BF), name="settle",
    )(recv, sums)


def local(gate, key, value, sf, taps, skip, gain, docs):
    place = lax.axis_index("ctx")
    width = lax.axis_size("ctx")
    ch, n = gate.shape
    base = (place * n).astype(jnp.int32).reshape(1)
    skip, gain = skip.reshape(1, ch), gain.reshape(1, ch)
    ends = tail(docs, base, gate, key, value, sf, skip, gain)
    halo = lax.ppermute(ends, "ctx", [(i, i + 1) for i in range(width - 1)])
    rows, squares = main(docs, base, gate, key, value, halo, sf, skip, gain, taps)
    recv = lax.all_to_all(rows.reshape(width, ch // width, n), "ctx", split_axis=0, concat_axis=0, tiled=True)
    total = lax.psum(jnp.sum(squares, axis=0, keepdims=True), "ch")
    sums = lax.all_to_all(jnp.broadcast_to(total[None], (width, 1, n)), "ctx", split_axis=0, concat_axis=0, tiled=True)
    return final(recv, sums)


def solution(mesh):
    in_specs = (P("ch", "ctx"),) * 3 + (P(None, None, "ch"), P("ch", None), P("ch"), P("ch"), P())
    return jax.shard_map(local, mesh=mesh, in_specs=in_specs, out_specs=P(("ch", "ctx"), None), check_vma=False)
```

```python
import functools

import jax
import jax.numpy as jnp
from jax import lax
from jax.experimental import pallas as pl
from jax.experimental.pallas import tpu as pltpu
from jax.sharding import PartitionSpec as P

D = 8192
GROUP = 16
MR = 128
EPS = 1e-6
DOCS = 64
F32 = jnp.float32
BF = jnp.bfloat16
CB = 128
ENDS = 144
SMEM = pl.BlockSpec(memory_space=pltpu.SMEM)


def starts_row(docs_ref, base, count):
    pos = lax.broadcasted_iota(jnp.int32, (1, count), 1) + base
    first = jnp.int32(0)
    start = jnp.zeros((1, count), jnp.int32)
    for d in range(DOCS):
        start = jnp.where(pos >= first, first, start)
        first = first + docs_ref[d]
    return pos, start


def set_keeps(keeps, pos, start):
    n = pos.shape[1]
    for lag in (1, 2):
        keeps[lag - 1] = jnp.broadcast_to((pos - lag >= start).astype(F32), (8, n))


def columns(sf, skip, gain):
    rows = [sf[0], sf[1], sf[2], skip, gain, jnp.zeros((5, CB), F32)]
    return jnp.concatenate(rows, axis=0).T


def conv3(ext, cols, first, keep):
    w = ext.shape[1] - 128
    one = pltpu.roll(ext, 1, 1)[:, 128:].reshape(CB // 8, 8, w) * keep[0][None]
    two = pltpu.roll(ext, 2, 1)[:, 128:].reshape(CB // 8, 8, w) * keep[1][None]
    return (cols[:, first:first + 1] * ext[:, 128:]
            + cols[:, first + 1:first + 2] * one.reshape(CB, w)
            + cols[:, first + 2:first + 3] * two.reshape(CB, w))


def tail_kernel(docs_ref, base_ref, gate_ref, key_ref, value_ref, sf_ref, out_ref, keeps):
    @pl.when(pl.program_id(0) == 0)
    def _():
        set_keeps(keeps, *starts_row(docs_ref, base_ref[0] + 384, 128))

    row = lax.broadcasted_iota(jnp.int32, (16, 128), 0)
    lane = lax.broadcasted_iota(jnp.int32, (16, 128), 1)
    for b in range(gate_ref.shape[0] // CB):
        here = slice(CB * b, CB * (b + 1))
        none = jnp.zeros((1, CB), F32)
        cols = columns(sf_ref[:, :, here], none, none)
        kc = conv3(key_ref[here].astype(F32), cols, 3, keeps)
        vc = conv3(value_ref[here].astype(F32), cols, 6, keeps)
        out_ref[b, :CB] = (kc * vc).astype(BF)
        raw = jnp.zeros((16, CB), F32)
        for i, ref in enumerate((gate_ref, key_ref, value_ref)):
            pick = ((lane == 126 + row - 2 * i) & (row >= 2 * i) & (row < 2 * i + 2)).astype(F32).astype(BF)
            raw = raw + lax.dot_general(pick, ref[here, 128:], (((1,), (1,)), ((), ())), preferred_element_type=F32)
        out_ref[b, CB:] = raw.astype(BF)


def main_kernel(later, docs_ref, base_ref, gate_ref, key_ref, value_ref, *refs):
    if later:
        sf_ref, skip_ref, gain_ref, taps_ref, out_ref, sq_ref, masks, keeps, prod, mixed, acc = refs
    else:
        (halo_ref, sq_later, _, sf_ref, skip_ref, gain_ref, taps_ref, out_ref, sq_ref,
         masks, keeps, prod, mixed, acc) = refs
    at = 256 if later else 0
    n = 256
    step = pl.program_id(0)

    @pl.when(step == 0)
    def _():
        base = base_ref[0] + at
        pos, start = starts_row(docs_ref, base - 128, n + 128)
        set_keeps(keeps, pos, start)
        s = lax.broadcasted_iota(jnp.int32, (128, 128), 0)
        t = lax.broadcasted_iota(jnp.int32, (128, 128), 1)
        for j in range(2):
            first = jnp.broadcast_to(start[:, 128 * (j + 1):128 * (j + 2)] - (base + 128 * j), (128, 128))
            masks[j, :128, :] = ((s > t) & (s - 128 >= first)).astype(F32).astype(BF)
            masks[j, 128:, :] = ((s <= t) & (s >= first)).astype(F32).astype(BF)
        acc[...] = jnp.zeros_like(acc)

    cols = columns(sf_ref[...], skip_ref[...], gain_ref[...])
    if later:
        kc = conv3(key_ref[...].astype(F32), cols, 3, keeps)
        vc = conv3(value_ref[...].astype(F32), cols, 6, keeps)
        prod[...] = (kc * vc).astype(BF)
        gate = gate_ref[:, 128:].astype(F32)
    else:
        row = lax.broadcasted_iota(jnp.int32, (16, 128), 0)
        lane = lax.broadcasted_iota(jnp.int32, (16, 128), 1)

        def before(i):
            put = ((lane == 126 + row - 2 * i) & (row >= 2 * i) & (row < 2 * i + 2)).astype(F32).astype(BF)
            return lax.dot_general(halo_ref[0, CB:], put, (((0,), (0,)), ((), ())), preferred_element_type=F32)

        keep = keeps[:, :, 128:]
        kc = conv3(jnp.concatenate([before(1), key_ref[...].astype(F32)], axis=1), cols, 3, keep)
        vc = conv3(jnp.concatenate([before(2), value_ref[...].astype(F32)], axis=1), cols, 6, keep)
        prod[:, :128] = halo_ref[0, :CB]
        prod[:, 128:] = (kc * vc).astype(BF)
        gate = jnp.concatenate([before(0), gate_ref[...].astype(F32)], axis=1)

    taps = taps_ref[...].astype(BF).astype(F32)
    for g in range(CB // GROUP):
        ring = pltpu.roll(jnp.broadcast_to(taps[g:g + 1], (128, 128)), 0, 1, stride=1, stride_axis=0).astype(BF)
        both = jnp.concatenate([ring, ring], axis=0)
        for j in range(2):
            mixed[GROUP * g:GROUP * (g + 1), 128 * j:128 * (j + 1)] = jnp.dot(
                prod[GROUP * g:GROUP * (g + 1), 128 * j:128 * j + 256], both * masks[j],
                preferred_element_type=F32)

    gc = conv3(gate, cols, 0, keeps[:, :, 128:])
    gated = gc * (mixed[...] + cols[:, 9:10] * prod[:, 128:].astype(F32))
    acc[...] += jnp.sum((gated * gated).reshape(CB // 8, 8, n), axis=0)
    out_ref[...] = (gated * cols[:, 10:11]).astype(BF)

    @pl.when(step == pl.num_programs(0) - 1)
    def _():
        row = jnp.sum(acc[...], axis=0, keepdims=True)
        sq_ref[...] = row if later else jnp.concatenate([row, sq_later[...]], axis=1)


def sf_spec(c):
    return pl.BlockSpec((3, 3, c), lambda i: (0, 0, i))


def tail(docs, base, gate, key, value, sf):
    ch, n = gate.shape
    c = min(512, ch)
    wide = pl.BlockSpec((c, 256), lambda i: (i, n // 256 - 1))
    return pl.pallas_call(
        tail_kernel, grid=(ch // c,),
        in_specs=[SMEM, SMEM, wide, wide, wide, sf_spec(c)],
        out_specs=pl.BlockSpec((c // CB, ENDS, 128), lambda i: (i, 0, 0)),
        out_shape=jax.ShapeDtypeStruct((ch // CB, ENDS, 128), BF),
        scratch_shapes=[pltpu.VMEM((2, 8, 128), F32)],
        compiler_params=pltpu.CompilerParams(vmem_limit_bytes=32 << 20), name="tail",
    )(docs, base, gate, key, value, sf)


def mixer(docs, base, gate, key, value, halo, earlier, sf, skip, gain, taps):
    ch, n = gate.shape
    later = halo is None
    row = pl.BlockSpec((1, CB), lambda i: (0, i))
    half = pl.BlockSpec((CB, 256), lambda i: (i, 0))
    raw = pl.BlockSpec((CB, n), lambda i: (i, 0)) if later else half
    extra, specs, alias = (), [], {}
    if not later:
        extra = (halo, earlier[1], earlier[0])
        specs = [pl.BlockSpec((1, ENDS, 128), lambda i: (i, 0, 0)), pl.BlockSpec((1, 256), lambda i: (0, 0)),
                 pl.BlockSpec(memory_space=pl.ANY)]
        alias = {7: 0}
    sq = 256 if later else 512
    return pl.pallas_call(
        functools.partial(main_kernel, later), grid=(ch // CB,),
        in_specs=[SMEM, SMEM, raw, raw, raw] + specs
        + [sf_spec(CB), row, row, pl.BlockSpec((CB // GROUP, MR), lambda i: (i, 0))],
        out_specs=[pl.BlockSpec((CB, 256), lambda i: (i, 1 if later else 0)), pl.BlockSpec((1, sq), lambda i: (0, 0))],
        out_shape=[jax.ShapeDtypeStruct((ch, n), BF), jax.ShapeDtypeStruct((1, sq), F32)],
        scratch_shapes=[pltpu.VMEM((2, 256, 128), BF), pltpu.VMEM((2, 8, 384), F32), pltpu.VMEM((CB, 384), BF),
                        pltpu.VMEM((CB, 256), F32), pltpu.VMEM((8, 256), F32)],
        input_output_aliases=alias,
        cost_estimate=pl.CostEstimate(flops=2 * ch * 256 * 256 * 8, bytes_accessed=6 * ch * 256, transcendentals=0),
        compiler_params=pltpu.CompilerParams(vmem_limit_bytes=32 << 20), name="later" if later else "first",
    )(docs, base, gate, key, value, *extra, sf, skip, gain, taps)


def final_kernel(recv_ref, sums_ref, out_ref):
    per, _, n = recv_ref.shape
    for i in range(per):
        scale = lax.rsqrt(sums_ref[i] / D + EPS)
        out_ref[:, n * i:n * (i + 1)] = (recv_ref[i].astype(F32) * scale).astype(BF)


def final(recv, sums):
    k, c, n = recv.shape
    per = min(k, 8)
    return pl.pallas_call(
        final_kernel, grid=(k // per,),
        in_specs=[pl.BlockSpec((per, c, n), lambda i: (i, 0, 0)), pl.BlockSpec((per, 1, n), lambda i: (i, 0, 0))],
        out_specs=pl.BlockSpec((c, per * n), lambda i: (0, i)),
        out_shape=jax.ShapeDtypeStruct((c, k * n), BF), name="settle",
    )(recv, sums)


def local(gate, key, value, sf, taps, skip, gain, docs):
    place = lax.axis_index("ctx")
    width = lax.axis_size("ctx")
    ch, n = gate.shape
    base = (place * n).astype(jnp.int32).reshape(1)
    skip, gain = skip.reshape(1, ch), gain.reshape(1, ch)
    ends = tail(docs, base, gate, key, value, sf)
    halo = lax.ppermute(ends, "ctx", [(i, i + 1) for i in range(width - 1)])
    later = mixer(docs, base, gate, key, value, None, None, sf, skip, gain, taps)
    rows, squares = mixer(docs, base, gate, key, value, halo, later, sf, skip, gain, taps)
    recv = lax.all_to_all(rows.reshape(width, ch // width, n), "ctx", split_axis=0, concat_axis=0, tiled=True)
    total = lax.psum(squares, "ch")
    total, recv = lax.optimization_barrier((total, recv))
    sums = lax.all_to_all(jnp.broadcast_to(total[None], (width, 1, n)), "ctx", split_axis=0, concat_axis=0, tiled=True)
    return final(recv, sums)


def solution(mesh):
    in_specs = (P("ch", "ctx"),) * 3 + (P(None, None, "ch"), P("ch", None), P("ch"), P("ch"), P())
    return jax.shard_map(local, mesh=mesh, in_specs=in_specs, out_specs=P(("ch", "ctx"), None), check_vma=False)
```

```python
import functools

import jax
import jax.numpy as jnp
from jax import lax
from jax.experimental import pallas as pl
from jax.experimental.pallas import tpu as pltpu
from jax.sharding import PartitionSpec as P

D = 8192
GROUP = 16
MR = 128
EPS = 1e-6
DOCS = 64
F32 = jnp.float32
BF = jnp.bfloat16
CB = 128
BL = 256
BIG = 56 << 20
PER = 16
ENDS = 144
SMEM = pl.BlockSpec(memory_space=pltpu.SMEM)


def starts_row(docs_ref, base, count):
    pos = lax.broadcasted_iota(jnp.int32, (1, count), 1) + base
    first = jnp.int32(0)
    start = jnp.zeros((1, count), jnp.int32)
    for d in range(DOCS):
        start = jnp.where(pos >= first, first, start)
        first = first + docs_ref[d]
    return pos, start


def set_keeps(keeps, pos, start):
    n = pos.shape[1]
    for lag in (1, 2):
        keeps[lag - 1] = jnp.broadcast_to((pos - lag >= start).astype(F32), (8, n))


def columns(sf, skip, gain):
    rows = [sf[0], sf[1], sf[2], skip, gain, jnp.zeros((5, CB), F32)]
    return jnp.concatenate(rows, axis=0).T


def conv3(ext, cols, first, keep):
    w = ext.shape[1] - 128
    one = pltpu.roll(ext, 1, 1)[:, 128:].reshape(CB // 8, 8, w) * keep[0][None]
    two = pltpu.roll(ext, 2, 1)[:, 128:].reshape(CB // 8, 8, w) * keep[1][None]
    return (cols[:, first:first + 1] * ext[:, 128:]
            + cols[:, first + 1:first + 2] * one.reshape(CB, w)
            + cols[:, first + 2:first + 3] * two.reshape(CB, w))


def tail_kernel(docs_ref, base_ref, gate_ref, key_ref, value_ref, sf_ref, out_ref, keeps):
    @pl.when(pl.program_id(0) == 0)
    def _():
        set_keeps(keeps, *starts_row(docs_ref, base_ref[0] + 384, 128))

    row = lax.broadcasted_iota(jnp.int32, (16, 128), 0)
    lane = lax.broadcasted_iota(jnp.int32, (16, 128), 1)
    for b in range(gate_ref.shape[0] // CB):
        here = slice(CB * b, CB * (b + 1))
        none = jnp.zeros((1, CB), F32)
        cols = columns(sf_ref[:, :, here], none, none)
        kc = conv3(key_ref[here].astype(F32), cols, 3, keeps)
        vc = conv3(value_ref[here].astype(F32), cols, 6, keeps)
        out_ref[b, :CB] = (kc * vc).astype(BF)
        raw = jnp.zeros((16, CB), F32)
        for i, ref in enumerate((gate_ref, key_ref, value_ref)):
            pick = ((lane == 126 + row - 2 * i) & (row >= 2 * i) & (row < 2 * i + 2)).astype(F32).astype(BF)
            raw = raw + lax.dot_general(pick, ref[here, 128:], (((1,), (1,)), ((), ())), preferred_element_type=F32)
        out_ref[b, CB:] = raw.astype(BF)


def block(later, b, gate_ref, key_ref, value_ref, halo_ref, sf_ref, skip_ref, gain_ref, taps_ref, out_ref,
          masks, keeps, prod, mixed, acc):
    n = 256
    here = slice(CB * b, CB * (b + 1))
    cols = columns(sf_ref[:, :, here], skip_ref[:, here], gain_ref[:, here])
    if later:
        kc = conv3(key_ref[here].astype(F32), cols, 3, keeps)
        vc = conv3(value_ref[here].astype(F32), cols, 6, keeps)
        prod[...] = (kc * vc).astype(BF)
        gate = gate_ref[here, 128:].astype(F32)
    else:
        row = lax.broadcasted_iota(jnp.int32, (16, 128), 0)
        lane = lax.broadcasted_iota(jnp.int32, (16, 128), 1)

        def before(i):
            put = ((lane == 126 + row - 2 * i) & (row >= 2 * i) & (row < 2 * i + 2)).astype(F32).astype(BF)
            return lax.dot_general(halo_ref[b, CB:], put, (((0,), (0,)), ((), ())), preferred_element_type=F32)

        keep = keeps[:, :, 128:]
        kc = conv3(jnp.concatenate([before(1), key_ref[here].astype(F32)], axis=1), cols, 3, keep)
        vc = conv3(jnp.concatenate([before(2), value_ref[here].astype(F32)], axis=1), cols, 6, keep)
        prod[:, :128] = halo_ref[b, :CB]
        prod[:, 128:] = (kc * vc).astype(BF)
        gate = jnp.concatenate([before(0), gate_ref[here].astype(F32)], axis=1)

    taps = taps_ref[8 * b:8 * (b + 1)].astype(BF).astype(F32)
    for g in range(CB // GROUP):
        ring = pltpu.roll(jnp.broadcast_to(taps[g:g + 1], (128, 128)), 0, 1, stride=1, stride_axis=0).astype(BF)
        both = jnp.concatenate([ring, ring], axis=0)
        for j in range(2):
            mixed[GROUP * g:GROUP * (g + 1), 128 * j:128 * (j + 1)] = jnp.dot(
                prod[GROUP * g:GROUP * (g + 1), 128 * j:128 * j + 256], both * masks[j],
                preferred_element_type=F32)

    gc = conv3(gate, cols, 0, keeps[:, :, 128:])
    gated = gc * (mixed[...] + cols[:, 9:10] * prod[:, 128:].astype(F32))
    acc[...] += jnp.sum((gated * gated).reshape(CB // 8, 8, n), axis=0)
    out_ref[here] = (gated * cols[:, 10:11]).astype(BF)


def main_kernel(later, docs_ref, base_ref, gate_ref, key_ref, value_ref, *refs):
    if later:
        sf_ref, skip_ref, gain_ref, taps_ref, out_ref, sq_ref, masks, keeps, prod, mixed, acc = refs
    else:
        (halo_ref, sq_later, _, sf_ref, skip_ref, gain_ref, taps_ref, out_ref, sq_ref,
         masks, keeps, prod, mixed, acc) = refs
    at = 256 if later else 0
    n = 256
    step = pl.program_id(0)

    @pl.when(step == 0)
    def _():
        base = base_ref[0] + at
        pos, start = starts_row(docs_ref, base - 128, n + 128)
        set_keeps(keeps, pos, start)
        s = lax.broadcasted_iota(jnp.int32, (128, 128), 0)
        t = lax.broadcasted_iota(jnp.int32, (128, 128), 1)
        for j in range(2):
            first = jnp.broadcast_to(start[:, 128 * (j + 1):128 * (j + 2)] - (base + 128 * j), (128, 128))
            masks[j, :128, :] = ((s > t) & (s - 128 >= first)).astype(F32).astype(BF)
            masks[j, 128:, :] = ((s <= t) & (s >= first)).astype(F32).astype(BF)
        acc[...] = jnp.zeros_like(acc)

    for b in range(gate_ref.shape[0] // CB):
        block(later, b, gate_ref, key_ref, value_ref, None if later else halo_ref, sf_ref, skip_ref, gain_ref, taps_ref,
              out_ref, masks, keeps, prod.at[b], mixed.at[b], acc)

    @pl.when(step == pl.num_programs(0) - 1)
    def _():
        row = jnp.sum(acc[...], axis=0, keepdims=True)
        sq_ref[...] = row if later else jnp.concatenate([row, sq_later[...]], axis=1)


def sf_spec(c):
    return pl.BlockSpec((3, 3, c), lambda i: (0, 0, i))


def tail(docs, base, gate, key, value, sf):
    ch, n = gate.shape
    c = min(512, ch)
    wide = pl.BlockSpec((c, 256), lambda i: (i, n // 256 - 1))
    return pl.pallas_call(
        tail_kernel, grid=(ch // c,),
        in_specs=[SMEM, SMEM, wide, wide, wide, sf_spec(c)],
        out_specs=pl.BlockSpec((c // CB, ENDS, 128), lambda i: (i, 0, 0)),
        out_shape=jax.ShapeDtypeStruct((ch // CB, ENDS, 128), BF),
        scratch_shapes=[pltpu.VMEM((2, 8, 128), F32)],
        compiler_params=pltpu.CompilerParams(vmem_limit_bytes=BIG), name="tail",
    )(docs, base, gate, key, value, sf)


def mixer(docs, base, gate, key, value, halo, earlier, sf, skip, gain, taps):
    ch, n = gate.shape
    later = halo is None
    bl = min(BL, ch)
    row = pl.BlockSpec((1, bl), lambda i: (0, i))
    half = pl.BlockSpec((bl, 256), lambda i: (i, 0))
    raw = pl.BlockSpec((bl, n), lambda i: (i, 0)) if later else half
    extra, specs, alias = (), [], {}
    if not later:
        extra = (halo, earlier[1], earlier[0])
        specs = [pl.BlockSpec((bl // CB, ENDS, 128), lambda i: (i, 0, 0)), pl.BlockSpec((1, 256), lambda i: (0, 0)),
                 pl.BlockSpec(memory_space=pl.ANY)]
        alias = {7: 0}
    sq = 256 if later else 512
    return pl.pallas_call(
        functools.partial(main_kernel, later), grid=(ch // bl,),
        in_specs=[SMEM, SMEM, raw, raw, raw] + specs
        + [sf_spec(bl), row, row, pl.BlockSpec((bl // GROUP, MR), lambda i: (i, 0))],
        out_specs=[pl.BlockSpec((bl, 256), lambda i: (i, 1 if later else 0)), pl.BlockSpec((1, sq), lambda i: (0, 0))],
        out_shape=[jax.ShapeDtypeStruct((ch, n), BF), jax.ShapeDtypeStruct((1, sq), F32)],
        scratch_shapes=[pltpu.VMEM((2, 256, 128), BF), pltpu.VMEM((2, 8, 384), F32), pltpu.VMEM((bl // CB, CB, 384), BF),
                        pltpu.VMEM((bl // CB, CB, 256), F32), pltpu.VMEM((8, 256), F32)],
        input_output_aliases=alias,
        cost_estimate=pl.CostEstimate(flops=2 * ch * 256 * 256 * 8, bytes_accessed=6 * ch * 256, transcendentals=0),
        compiler_params=pltpu.CompilerParams(vmem_limit_bytes=BIG), name="later" if later else "first",
    )(docs, base, gate, key, value, *extra, sf, skip, gain, taps)


def final_kernel(recv_ref, sums_ref, out_ref):
    per, _, n = recv_ref.shape
    for i in range(per):
        scale = lax.rsqrt(sums_ref[i] / D + EPS)
        out_ref[:, n * i:n * (i + 1)] = (recv_ref[i].astype(F32) * scale).astype(BF)


def final(recv, sums):
    k, c, n = recv.shape
    per = min(k, PER)
    return pl.pallas_call(
        final_kernel, grid=(k // per,),
        in_specs=[pl.BlockSpec((per, c, n), lambda i: (i, 0, 0)), pl.BlockSpec((per, 1, n), lambda i: (i, 0, 0))],
        out_specs=pl.BlockSpec((c, per * n), lambda i: (0, i)),
        out_shape=jax.ShapeDtypeStruct((c, k * n), BF),
        compiler_params=pltpu.CompilerParams(vmem_limit_bytes=BIG), name="settle",
    )(recv, sums)


ROUNDS = (((0, 1), (2, 3), (4, 5), (6, 7)), ((1, 2), (3, 4), (5, 6), (7, 0)), ((0, 3), (7, 4), (1, 6), (2, 5)))


def channel_sum(x):
    if lax.axis_size("ch") != 8:
        return lax.psum(x, "ch")
    for pairs in ROUNDS:
        x = x + lax.ppermute(x, "ch", list(pairs) + [(b, a) for a, b in pairs])
    return x


def local(gate, key, value, sf, taps, skip, gain, docs):
    place = lax.axis_index("ctx")
    width = lax.axis_size("ctx")
    ch, n = gate.shape
    base = (place * n).astype(jnp.int32).reshape(1)
    skip, gain = skip.reshape(1, ch), gain.reshape(1, ch)
    ends = tail(docs, base, gate, key, value, sf)
    halo = lax.ppermute(ends, "ctx", [(i, i + 1) for i in range(width - 1)])
    later = mixer(docs, base, gate, key, value, None, None, sf, skip, gain, taps)
    rows, squares = mixer(docs, base, gate, key, value, halo, later, sf, skip, gain, taps)
    recv = lax.all_to_all(rows.reshape(width, ch // width, n), "ctx", split_axis=0, concat_axis=0, tiled=True)
    total = channel_sum(squares)
    total, recv = lax.optimization_barrier((total, recv))
    sums = lax.all_to_all(jnp.broadcast_to(total[None], (width, 1, n)), "ctx", split_axis=0, concat_axis=0, tiled=True)
    return final(recv, sums)


def solution(mesh):
    in_specs = (P("ch", "ctx"),) * 3 + (P(None, None, "ch"), P("ch", None), P("ch"), P("ch"), P())
    return jax.shard_map(local, mesh=mesh, in_specs=in_specs, out_specs=P(("ch", "ctx"), None), check_vma=False)
```

```python
import jax
import jax.numpy as jnp
from jax import lax
from jax.experimental import pallas as pl
from jax.experimental.pallas import tpu as pltpu
from jax.sharding import PartitionSpec as P

D = 8192
GROUP = 16
MR = 128
EPS = 1e-6
DOCS = 64
F32 = jnp.float32
BF = jnp.bfloat16
CB = 128
BL = 512
ENDS = 144
PER = 16
BIG = 56 << 20
SMEM = pl.BlockSpec(memory_space=pltpu.SMEM)


def starts_row(docs_ref, base, count):
    pos = lax.broadcasted_iota(jnp.int32, (1, count), 1) + base
    first = jnp.int32(0)
    start = jnp.zeros((1, count), jnp.int32)
    for d in range(DOCS):
        start = jnp.where(pos >= first, first, start)
        first = first + docs_ref[d]
    return pos, start


def as_bf(flag, shape):
    return jnp.broadcast_to(flag.astype(F32), shape).astype(BF)


def tile_masks(first):
    s = lax.broadcasted_iota(jnp.int32, (128, 128), 0)
    t = lax.broadcasted_iota(jnp.int32, (128, 128), 1)
    return (((s > t) & (s - 128 >= first)).astype(F32).astype(BF), ((s <= t) & (s >= first)).astype(F32).astype(BF))


def columns(rows):
    rows = rows + [jnp.zeros((16 - sum(r.shape[0] for r in rows), CB), F32)]
    return jnp.concatenate(rows, axis=0).T


def conv3(raw, keeps, cols, first):
    one = pltpu.roll(raw, 1, 1) * keeps[0]
    two = pltpu.roll(raw, 2, 1) * keeps[1]
    return (cols[:, first:first + 1] * raw.astype(F32) + cols[:, first + 1:first + 2] * one.astype(F32)
            + cols[:, first + 2:first + 3] * two.astype(F32))


def ring_of(taps):
    return pltpu.roll(jnp.broadcast_to(taps, (128, 128)), 0, 1, stride=1, stride_axis=0).astype(BF)


def pick(here, *wanted):
    row = lax.broadcasted_iota(jnp.int32, (16, 128), 0)
    lane = lax.broadcasted_iota(jnp.int32, (16, 128), 1)
    out = jnp.zeros((16, CB), F32)
    for ref, lanes, at, first, count in wanted:
        one_hot = ((lane - first == row - at) & (row >= at) & (row < at + count)).astype(F32).astype(BF)
        out = out + lax.dot_general(one_hot, ref[here, lanes], (((1,), (1,)), ((), ())), preferred_element_type=F32)
    return out.astype(BF)


def tail_kernel(docs_ref, base_ref, gate_ref, key_ref, value_ref, sf_ref, out_ref, keeps):
    @pl.when(pl.program_id(0) == 0)
    def _():
        pos, start = starts_row(docs_ref, base_ref[0] + 384, 128)
        for lag in (1, 2):
            keeps[lag - 1] = as_bf(pos - lag >= start, (GROUP, 128))

    last = lax.broadcasted_iota(jnp.int32, (GROUP, 128), 1) == 127

    def filtered(ref, at, cols, i):
        raw = ref[at, 128:]
        one = pltpu.roll(raw, 1, 1) * keeps[0]
        two = pltpu.roll(jnp.where(last, ref[at, :128], raw), 2, 1) * keeps[1]
        return (cols[:, i:i + 1] * raw.astype(F32) + cols[:, i + 1:i + 2] * one.astype(F32)
                + cols[:, i + 2:i + 3] * two.astype(F32))

    for b in range(gate_ref.shape[0] // CB):
        here = slice(CB * b, CB * (b + 1))
        sf = sf_ref[:, :, here]
        cols = columns([sf[1], sf[2]])
        for g in range(CB // GROUP):
            at = slice(CB * b + GROUP * g, CB * b + GROUP * (g + 1))
            c = cols[GROUP * g:GROUP * (g + 1)]
            out_ref[b, GROUP * g:GROUP * (g + 1)] = (filtered(key_ref, at, c, 0) * filtered(value_ref, at, c, 3)).astype(BF)
        lanes = slice(128, 256)
        out_ref[b, CB:] = pick(here, (gate_ref, lanes, 0, 126, 2), (key_ref, lanes, 2, 126, 2), (value_ref, lanes, 4, 126, 2))


def later_kernel(docs_ref, base_ref, gate_ref, key_ref, value_ref, sf_ref, skip_ref, taps_ref,
                 out_ref, aux_ref, prod_ref, own_ref, ring_ref, sq_ref, masks, keeps, inner, acc):
    step = pl.program_id(0)

    @pl.when(step == 0)
    def _():
        pos, start = starts_row(docs_ref, base_ref[0], 512)
        rel = pos - base_ref[0]
        for lag in (1, 2):
            keeps[lag - 1] = as_bf((pos - lag >= start) & (rel >= lag), (GROUP, 512))
        inner[...] = as_bf(rel[:, :128] >= 2, (GROUP, 128))
        for j in range(3):
            first = start[:, 128 * (j + 1):128 * (j + 2)] - (base_ref[0] + 128 * (j + 1))
            masks[j, :128, :], masks[j, 128:, :] = tile_masks(jnp.broadcast_to(first, (128, 128)))
        acc[...] = jnp.zeros_like(acc)

    total = acc[...]
    for b in range(gate_ref.shape[0] // CB):
        here = slice(CB * b, CB * (b + 1))
        sf = sf_ref[:, :, here]
        cols = columns([sf[0], sf[1], sf[2], skip_ref[:, here]])
        taps = taps_ref[8 * b:8 * (b + 1)].astype(BF).astype(F32)
        for g in range(CB // GROUP):
            at = slice(CB * b + GROUP * g, CB * b + GROUP * (g + 1))
            c = cols[GROUP * g:GROUP * (g + 1)]
            product = (conv3(key_ref[at], keeps, c, 3) * conv3(value_ref[at], keeps, c, 6)).astype(BF)
            product = jnp.concatenate([product[:, :128] * inner[...], product[:, 128:]], axis=1)
            prod_ref[at] = product[:, :128]
            gate = conv3(gate_ref[at], keeps, c, 0)
            ring = ring_of(taps[g:g + 1])
            ring_ref[8 * b + g] = ring
            both = jnp.concatenate([ring, ring], axis=0)
            mixed = jnp.concatenate([
                jnp.dot(product[:, 128 * j:128 * j + 256], both * masks[j], preferred_element_type=F32)
                for j in range(3)], axis=1)
            mixed = mixed + c[:, 9:10] * product[:, 128:].astype(F32)
            gated = gate[:, 128:] * mixed
            aux_ref[at] = gate[:, :128]
            square = gated * gated
            total = total + square[:8] + square[8:]
            out_ref[at, 128:] = gated.astype(BF)
            out_ref[at, :128] = jnp.zeros((GROUP, 128), BF)
        tile0, tile1 = slice(0, 128), slice(128, 256)
        own_ref[b] = pick(here, (gate_ref, tile0, 0, 0, 2), (key_ref, tile0, 2, 0, 2), (value_ref, tile0, 4, 0, 2),
                          (gate_ref, tile0, 6, 126, 2), (gate_ref, tile1, 8, 0, 1))
    acc[...] = total

    @pl.when(step == pl.num_programs(0) - 1)
    def _():
        sq_ref[...] = jnp.sum(acc[...], axis=0, keepdims=True)


def first_kernel(docs_ref, base_ref, halo_ref, rows_ref, aux_ref, prod_ref, own_ref, ring_ref, later_ref, sf_ref, skip_ref,
                 taps_ref, out_ref, sq_ref, masks, keeps, acc):
    step = pl.program_id(0)

    @pl.when(step == 0)
    def _():
        pos, start = starts_row(docs_ref, base_ref[0], 256)
        for lag in (1, 2):
            keeps[lag - 1:lag] = (pos[:, :128] - lag >= start[:, :128]).astype(F32)
        for lag in (1, 2, 127):
            row = 1 + lag if lag < 3 else 4
            keeps[row:row + 1] = (pos[:, 128:] - lag >= start[:, 128:]).astype(F32)
        masks[:128], masks[128:] = tile_masks(jnp.broadcast_to(start[:, :128] - base_ref[0], (128, 128)))
        acc[...] = jnp.zeros_like(acc)

    lane = lax.broadcasted_iota(jnp.int32, (GROUP, 128), 1)
    one_hot = (lax.broadcasted_iota(jnp.int32, (16, 128), 0) == lane).astype(F32).astype(BF)
    total0, total1 = acc[0], acc[1]
    for b in range(halo_ref.shape[0]):
        here = slice(CB * b, CB * (b + 1))
        own = own_ref[b].astype(F32)
        past = halo_ref[b, CB:].astype(F32)

        def both_positions(i):
            t = [sf_ref[i, lag:lag + 1, here] for lag in range(3)]
            x = own[2 * i:2 * i + 2]
            h = past[2 * i:2 * i + 2]
            at0 = t[0] * x[:1] + keeps[0:1, 0:1] * (t[1] * h[1:]) + keeps[1:2, 0:1] * (t[2] * h[:1])
            at1 = t[0] * x[1:] + keeps[0:1, 1:2] * (t[1] * x[:1]) + keeps[1:2, 1:2] * (t[2] * h[1:])
            return jnp.concatenate([at0, at1], axis=0)

        two = (both_positions(1) * both_positions(2)).astype(BF).astype(F32)
        t = [sf_ref[0, lag:lag + 1, here] for lag in range(3)]
        gate = t[0] * own[8:9] + keeps[2:3, 0:1] * (t[1] * own[7:8]) + keeps[3:4, 0:1] * (t[2] * own[6:7])
        cols = columns([skip_ref[:, here], both_positions(0), keeps[4:5, 0:1] * two[1:] * gate])
        put = lax.dot_general(jnp.concatenate([two, jnp.zeros((14, CB), F32)], axis=0).astype(BF), one_hot,
                              (((0,), (0,)), ((), ())), preferred_element_type=F32)
        taps = taps_ref[8 * b:8 * (b + 1)].astype(BF).astype(F32)
        for g in range(CB // GROUP):
            at = slice(CB * b + GROUP * g, CB * b + GROUP * (g + 1))
            inside = slice(GROUP * g, GROUP * (g + 1))
            c = cols[inside]
            product = prod_ref[at] + put[inside].astype(BF)
            ring = ring_ref[8 * b + g]
            mixed = jnp.dot(jnp.concatenate([halo_ref[b, inside], product], axis=1),
                            jnp.concatenate([ring, ring], axis=0) * masks[...], preferred_element_type=F32)
            mixed = mixed + c[:, 0:1] * product.astype(F32)
            gated = jnp.where(lane == 0, c[:, 1:2], jnp.where(lane == 1, c[:, 2:3], aux_ref[at])) * mixed
            old = rows_ref[at, 128:].astype(F32)
            after = jnp.where(lane == 0, old + c[:, 3:4] * taps[g:g + 1, 127:128], old)
            square = gated * gated
            total0 = total0 + square[:8] + square[8:]
            square = after * after
            total1 = total1 + square[:8] + square[8:]
            out_ref[at, :128] = gated.astype(BF)
            out_ref[at, 128:] = after.astype(BF)
    acc[0], acc[1] = total0, total1

    @pl.when(step == pl.num_programs(0) - 1)
    def _():
        row0 = jnp.sum(acc[0], axis=0, keepdims=True)
        row1 = jnp.sum(acc[1], axis=0, keepdims=True)
        one = lax.broadcasted_iota(jnp.int32, (1, 128), 1)
        sq_ref[...] = jnp.concatenate(
            [row0, jnp.where(one == 0, row1, later_ref[:, :128]), later_ref[:, 128:]], axis=1)


def sf_spec(c):
    return pl.BlockSpec((3, 3, c), lambda i: (0, 0, i))


def tail(docs, base, gate, key, value, sf):
    ch, n = gate.shape
    c = min(BL, ch)
    wide = pl.BlockSpec((c, 256), lambda i: (i, n // 256 - 1))
    return pl.pallas_call(
        tail_kernel, grid=(ch // c,),
        in_specs=[SMEM, SMEM, wide, wide, wide, sf_spec(c)],
        out_specs=pl.BlockSpec((c // CB, ENDS, 128), lambda i: (i, 0, 0)),
        out_shape=jax.ShapeDtypeStruct((ch // CB, ENDS, 128), BF),
        scratch_shapes=[pltpu.VMEM((2, GROUP, 128), BF)],
        compiler_params=pltpu.CompilerParams(vmem_limit_bytes=BIG), name="tail",
    )(docs, base, gate, key, value, sf)


def param_specs(c):
    row = pl.BlockSpec((1, c), lambda i: (0, i))
    return [sf_spec(c), row, pl.BlockSpec((c // GROUP, MR), lambda i: (i, 0))]


def later(docs, base, gate, key, value, sf, skip, taps):
    ch, n = gate.shape
    c = min(BL, ch)
    wide = pl.BlockSpec((c, n), lambda i: (i, 0))
    tile = pl.BlockSpec((c, 128), lambda i: (i, 0))
    return pl.pallas_call(
        later_kernel, grid=(ch // c,),
        in_specs=[SMEM, SMEM, wide, wide, wide] + param_specs(c),
        out_specs=[wide, tile, tile, pl.BlockSpec((c // CB, 16, CB), lambda i: (i, 0, 0)),
                   pl.BlockSpec((c // GROUP, MR, MR), lambda i: (i, 0, 0)), pl.BlockSpec((1, n - 128), lambda i: (0, 0))],
        out_shape=[jax.ShapeDtypeStruct((ch, n), BF), jax.ShapeDtypeStruct((ch, 128), F32),
                   jax.ShapeDtypeStruct((ch, 128), BF), jax.ShapeDtypeStruct((ch // CB, 16, CB), BF),
                   jax.ShapeDtypeStruct((ch // GROUP, MR, MR), BF), jax.ShapeDtypeStruct((1, n - 128), F32)],
        scratch_shapes=[pltpu.VMEM((3, 256, 128), BF), pltpu.VMEM((2, GROUP, n), BF), pltpu.VMEM((GROUP, 128), BF),
                        pltpu.VMEM((8, n - 128), F32)],
        cost_estimate=pl.CostEstimate(flops=2 * ch * 384 * 256 * 8, bytes_accessed=8 * ch * n, transcendentals=0),
        compiler_params=pltpu.CompilerParams(vmem_limit_bytes=BIG), name="later",
    )(docs, base, gate, key, value, sf, skip, taps)


def first(docs, base, halo, done, sf, skip, taps):
    rows, aux, prod, own, rings, squares = done
    ch, n = rows.shape
    c = min(BL, ch)
    half = pl.BlockSpec((c, 256), lambda i: (i, 0))
    tile = pl.BlockSpec((c, 128), lambda i: (i, 0))
    whole = lambda w: pl.BlockSpec((1, w), lambda i: (0, 0))
    return pl.pallas_call(
        first_kernel, grid=(ch // c,),
        in_specs=[SMEM, SMEM, pl.BlockSpec((c // CB, ENDS, 128), lambda i: (i, 0, 0)), half, tile, tile,
                  pl.BlockSpec((c // CB, 16, CB), lambda i: (i, 0, 0)),
                  pl.BlockSpec((c // GROUP, MR, MR), lambda i: (i, 0, 0)), whole(n - 128)] + param_specs(c),
        out_specs=[half, whole(n)],
        out_shape=[jax.ShapeDtypeStruct((ch, n), BF), jax.ShapeDtypeStruct((1, n), F32)],
        scratch_shapes=[pltpu.VMEM((256, 128), BF), pltpu.VMEM((8, 128), F32), pltpu.VMEM((2, 8, 128), F32)],
        input_output_aliases={3: 0},
        cost_estimate=pl.CostEstimate(flops=2 * ch * 128 * 256 * 8, bytes_accessed=4 * ch * n, transcendentals=0),
        compiler_params=pltpu.CompilerParams(vmem_limit_bytes=FIRST_VMEM), name="first",
    )(docs, base, halo, rows, aux, prod, own, rings, squares, sf, skip, taps)


FIRST_VMEM = 56 << 20
def final_kernel(recv_ref, sums_ref, gain_ref, out_ref):
    per, c, n = recv_ref.shape
    gain = jnp.broadcast_to(gain_ref[...], (c, n))
    for i in range(per):
        scale = lax.rsqrt(sums_ref[i] / D + EPS)
        out_ref[:, n * i:n * (i + 1)] = (recv_ref[i].astype(F32) * scale * gain).astype(BF)


def final(recv, sums, gain):
    k, c, n = recv.shape
    per = min(k, PER)
    return pl.pallas_call(
        final_kernel, grid=(k // per,),
        in_specs=[pl.BlockSpec((per, c, n), lambda i: (i, 0, 0)), pl.BlockSpec((per, 1, n), lambda i: (i, 0, 0)),
                  pl.BlockSpec((c, 1), lambda i: (0, 0))],
        out_specs=pl.BlockSpec((c, per * n), lambda i: (0, i)),
        out_shape=jax.ShapeDtypeStruct((c, k * n), BF),
        compiler_params=pltpu.CompilerParams(vmem_limit_bytes=24 << 20), name="settle",
    )(recv, sums, gain)


ROUNDS = (((0, 1), (2, 3), (4, 5), (6, 7)), ((1, 2), (3, 4), (5, 6), (7, 0)), ((0, 3), (7, 4), (1, 6), (2, 5)))


def channel_sum(x):
    if lax.axis_size("ch") != 8:
        return lax.psum(x, "ch")
    for pairs in ROUNDS:
        x = x + lax.ppermute(x, "ch", list(pairs) + [(b, a) for a, b in pairs])
    return x


def local(gate, key, value, sf, taps, skip, gain, docs):
    place = lax.axis_index("ctx")
    width = lax.axis_size("ctx")
    ch, n = gate.shape
    base = (place * n).astype(jnp.int32).reshape(1)
    skip = skip.reshape(1, ch)
    gain = lax.dynamic_slice_in_dim(gain, place * (ch // width), ch // width).reshape(ch // width, 1)
    ends = tail(docs, base, gate, key, value, sf)
    halo = lax.ppermute(ends, "ctx", [(i, i + 1) for i in range(width - 1)])
    done = later(docs, base, gate, key, value, sf, skip, taps)
    rows, squares = first(docs, base, halo, done, sf, skip, taps)
    recv = lax.all_to_all(rows.reshape(width, ch // width, n), "ctx", split_axis=0, concat_axis=0, tiled=True)
    total = channel_sum(squares)
    total, recv = lax.optimization_barrier((total, recv))
    sums = lax.all_to_all(jnp.broadcast_to(total[None], (width, 1, n)), "ctx", split_axis=0, concat_axis=0, tiled=True)
    return final(recv, sums, gain)


def solution(mesh):
    in_specs = (P("ch", "ctx"),) * 3 + (P(None, None, "ch"), P("ch", None), P("ch"), P("ch"), P())
    return jax.shard_map(local, mesh=mesh, in_specs=in_specs, out_specs=P(("ch", "ctx"), None), check_vma=False)
```

```python
import jax
import jax.numpy as jnp
from jax import lax
from jax.experimental import pallas as pl
from jax.experimental.pallas import tpu as pltpu
from jax.sharding import PartitionSpec as P

D = 8192
GROUP = 16
MR = 128
EPS = 1e-6
DOCS = 64
F32 = jnp.float32
BF = jnp.bfloat16
CB = 128
BL = 512
ENDS = 144
PER = 16
BIG = 56 << 20
SMEM = pl.BlockSpec(memory_space=pltpu.SMEM)


def starts_row(docs_ref, base, count):
    pos = lax.broadcasted_iota(jnp.int32, (1, count), 1) + base
    first = jnp.int32(0)
    start = jnp.zeros((1, count), jnp.int32)
    for d in range(DOCS):
        start = jnp.where(pos >= first, first, start)
        first = first + docs_ref[d]
    return pos, start


def as_bf(flag, shape):
    return jnp.broadcast_to(flag.astype(F32), shape).astype(BF)


def tile_masks(first):
    s = lax.broadcasted_iota(jnp.int32, (128, 128), 0)
    t = lax.broadcasted_iota(jnp.int32, (128, 128), 1)
    return (((s > t) & (s - 128 >= first)).astype(F32).astype(BF), ((s <= t) & (s >= first)).astype(F32).astype(BF))


def spread(rows):
    count = sum(r.shape[0] for r in rows)
    rest = jnp.concatenate(rows + [jnp.zeros((16 - count, CB), F32)], axis=0)
    pieces = []
    for _ in range(3):
        pieces.append(rest.astype(BF))
        rest = rest - pieces[-1].astype(F32)
    row = lax.broadcasted_iota(jnp.int32, (16, 128 * count), 0)
    column = lax.broadcasted_iota(jnp.int32, (16, 128 * count), 1)
    ones = ((column >= 128 * row) & (column < 128 * row + 128)).astype(F32).astype(BF)
    return lax.dot_general(jnp.concatenate(pieces, axis=0), jnp.concatenate([ones] * 3, axis=0),
                           (((0,), (0,)), ((), ())), preferred_element_type=F32)


def lanes_of(wide, i, tiles=1):
    part = wide[:, 128 * i:128 * (i + 1)]
    return part if tiles == 1 else jnp.concatenate([part] * tiles, axis=1)


def conv3(raw, keeps, cols, first):
    one = pltpu.roll(raw, 1, 1) * keeps[0]
    two = pltpu.roll(raw, 2, 1) * keeps[1]
    k = raw.shape[1] // 128
    return (lanes_of(cols, first, k) * raw.astype(F32) + lanes_of(cols, first + 1, k) * one.astype(F32)
            + lanes_of(cols, first + 2, k) * two.astype(F32))


def ring_of(taps):
    return pltpu.roll(jnp.broadcast_to(taps, (128, 128)), 0, 1, stride=1, stride_axis=0).astype(BF)


def pick(here, *wanted):
    row = lax.broadcasted_iota(jnp.int32, (16, 128), 0)
    lane = lax.broadcasted_iota(jnp.int32, (16, 128), 1)
    out = jnp.zeros((16, CB), F32)
    for ref, lanes, at, first, count in wanted:
        one_hot = ((lane - first == row - at) & (row >= at) & (row < at + count)).astype(F32).astype(BF)
        out = out + lax.dot_general(one_hot, ref[here, lanes], (((1,), (1,)), ((), ())), preferred_element_type=F32)
    return out.astype(BF)


def tail_kernel(docs_ref, base_ref, gate_ref, key_ref, value_ref, sf_ref, out_ref, keeps):
    @pl.when(pl.program_id(0) == 0)
    def _():
        pos, start = starts_row(docs_ref, base_ref[0] + 384, 128)
        for lag in (1, 2):
            keeps[lag - 1] = as_bf(pos - lag >= start, (GROUP, 128))

    last = lax.broadcasted_iota(jnp.int32, (GROUP, 128), 1) == 127

    def filtered(ref, at, cols, i):
        raw = ref[at, 128:]
        one = pltpu.roll(raw, 1, 1) * keeps[0]
        two = pltpu.roll(jnp.where(last, ref[at, :128], raw), 2, 1) * keeps[1]
        return (lanes_of(cols, i) * raw.astype(F32) + lanes_of(cols, i + 1) * one.astype(F32)
                + lanes_of(cols, i + 2) * two.astype(F32))

    for b in range(gate_ref.shape[0] // CB):
        here = slice(CB * b, CB * (b + 1))
        sf = sf_ref[:, :, here]
        cols = spread([sf[1], sf[2]])
        for g in range(CB // GROUP):
            at = slice(CB * b + GROUP * g, CB * b + GROUP * (g + 1))
            c = cols[GROUP * g:GROUP * (g + 1)]
            out_ref[b, GROUP * g:GROUP * (g + 1)] = (filtered(key_ref, at, c, 0) * filtered(value_ref, at, c, 3)).astype(BF)
        lanes = slice(128, 256)
        out_ref[b, CB:] = pick(here, (gate_ref, lanes, 0, 126, 2), (key_ref, lanes, 2, 126, 2), (value_ref, lanes, 4, 126, 2))


def later_kernel(docs_ref, base_ref, gate_ref, key_ref, value_ref, sf_ref, skip_ref, taps_ref,
                 out_ref, aux_ref, prod_ref, own_ref, ring_ref, sq_ref, masks, keeps, inner, acc):
    step = pl.program_id(0)

    @pl.when(step == 0)
    def _():
        pos, start = starts_row(docs_ref, base_ref[0], 512)
        rel = pos - base_ref[0]
        for lag in (1, 2):
            keeps[lag - 1] = as_bf((pos - lag >= start) & (rel >= lag), (GROUP, 512))
        inner[...] = as_bf(rel[:, :128] >= 2, (GROUP, 128))
        for j in range(3):
            first = start[:, 128 * (j + 1):128 * (j + 2)] - (base_ref[0] + 128 * (j + 1))
            masks[j, :128, :], masks[j, 128:, :] = tile_masks(jnp.broadcast_to(first, (128, 128)))
        acc[...] = jnp.zeros_like(acc)

    total = acc[...]
    for b in range(gate_ref.shape[0] // CB):
        here = slice(CB * b, CB * (b + 1))
        sf = sf_ref[:, :, here]
        cols = spread([sf[0], sf[1], sf[2], skip_ref[:, here]])
        taps = taps_ref[8 * b:8 * (b + 1)].astype(BF).astype(F32)
        for g in range(CB // GROUP):
            at = slice(CB * b + GROUP * g, CB * b + GROUP * (g + 1))
            c = cols[GROUP * g:GROUP * (g + 1)]
            product = (conv3(key_ref[at], keeps, c, 3) * conv3(value_ref[at], keeps, c, 6)).astype(BF)
            product = jnp.concatenate([product[:, :128] * inner[...], product[:, 128:]], axis=1)
            prod_ref[at] = product[:, :128]
            gate = conv3(gate_ref[at], keeps, c, 0)
            ring = ring_of(taps[g:g + 1])
            ring_ref[8 * b + g] = ring
            both = jnp.concatenate([ring, ring], axis=0)
            mixed = jnp.concatenate([
                jnp.dot(product[:, 128 * j:128 * j + 256], both * masks[j], preferred_element_type=F32)
                for j in range(3)], axis=1)
            mixed = mixed + lanes_of(c, 9, 3) * product[:, 128:].astype(F32)
            gated = gate[:, 128:] * mixed
            aux_ref[at] = gate[:, :128]
            square = gated * gated
            total = total + square[:8] + square[8:]
            out_ref[at, 128:] = gated.astype(BF)
            out_ref[at, :128] = jnp.zeros((GROUP, 128), BF)
        tile0, tile1 = slice(0, 128), slice(128, 256)
        own_ref[b] = pick(here, (gate_ref, tile0, 0, 0, 2), (key_ref, tile0, 2, 0, 2), (value_ref, tile0, 4, 0, 2),
                          (gate_ref, tile0, 6, 126, 2), (gate_ref, tile1, 8, 0, 1))
    acc[...] = total

    @pl.when(step == pl.num_programs(0) - 1)
    def _():
        sq_ref[...] = jnp.sum(acc[...], axis=0, keepdims=True)


def first_kernel(docs_ref, base_ref, halo_ref, rows_ref, aux_ref, prod_ref, own_ref, ring_ref, later_ref, sf_ref, skip_ref,
                 taps_ref, out_ref, sq_ref, masks, keeps, acc):
    step = pl.program_id(0)

    @pl.when(step == 0)
    def _():
        pos, start = starts_row(docs_ref, base_ref[0], 256)
        for lag in (1, 2):
            keeps[lag - 1:lag] = (pos[:, :128] - lag >= start[:, :128]).astype(F32)
        for lag in (1, 2, 127):
            row = 1 + lag if lag < 3 else 4
            keeps[row:row + 1] = (pos[:, 128:] - lag >= start[:, 128:]).astype(F32)
        masks[:128], masks[128:] = tile_masks(jnp.broadcast_to(start[:, :128] - base_ref[0], (128, 128)))
        acc[...] = jnp.zeros_like(acc)

    lane = lax.broadcasted_iota(jnp.int32, (GROUP, 128), 1)
    one_hot = (lax.broadcasted_iota(jnp.int32, (16, 128), 0) == lane).astype(F32).astype(BF)
    total0, total1 = acc[0], acc[1]
    for b in range(halo_ref.shape[0]):
        here = slice(CB * b, CB * (b + 1))
        own = own_ref[b].astype(F32)
        past = halo_ref[b, CB:].astype(F32)

        def both_positions(i):
            t = [sf_ref[i, lag:lag + 1, here] for lag in range(3)]
            x = own[2 * i:2 * i + 2]
            h = past[2 * i:2 * i + 2]
            at0 = t[0] * x[:1] + keeps[0:1, 0:1] * (t[1] * h[1:]) + keeps[1:2, 0:1] * (t[2] * h[:1])
            at1 = t[0] * x[1:] + keeps[0:1, 1:2] * (t[1] * x[:1]) + keeps[1:2, 1:2] * (t[2] * h[1:])
            return jnp.concatenate([at0, at1], axis=0)

        two = (both_positions(1) * both_positions(2)).astype(BF).astype(F32)
        t = [sf_ref[0, lag:lag + 1, here] for lag in range(3)]
        gate = t[0] * own[8:9] + keeps[2:3, 0:1] * (t[1] * own[7:8]) + keeps[3:4, 0:1] * (t[2] * own[6:7])
        cols = spread([skip_ref[:, here], both_positions(0), keeps[4:5, 0:1] * two[1:] * gate])
        put = lax.dot_general(jnp.concatenate([two, jnp.zeros((14, CB), F32)], axis=0).astype(BF), one_hot,
                              (((0,), (0,)), ((), ())), preferred_element_type=F32)
        taps = taps_ref[8 * b:8 * (b + 1)].astype(BF).astype(F32)
        for g in range(CB // GROUP):
            at = slice(CB * b + GROUP * g, CB * b + GROUP * (g + 1))
            inside = slice(GROUP * g, GROUP * (g + 1))
            c = cols[inside]
            product = prod_ref[at] + put[inside].astype(BF)
            ring = ring_ref[8 * b + g]
            mixed = jnp.dot(jnp.concatenate([halo_ref[b, inside], product], axis=1),
                            jnp.concatenate([ring, ring], axis=0) * masks[...], preferred_element_type=F32)
            mixed = mixed + lanes_of(c, 0) * product.astype(F32)
            gated = jnp.where(lane == 0, lanes_of(c, 1), jnp.where(lane == 1, lanes_of(c, 2), aux_ref[at])) * mixed
            old = rows_ref[at, 128:].astype(F32)
            after = jnp.where(lane == 0, old + lanes_of(c, 3) * taps[g:g + 1, 127:128], old)
            square = gated * gated
            total0 = total0 + square[:8] + square[8:]
            square = after * after
            total1 = total1 + square[:8] + square[8:]
            out_ref[at, :128] = gated.astype(BF)
            out_ref[at, 128:] = after.astype(BF)
    acc[0], acc[1] = total0, total1

    @pl.when(step == pl.num_programs(0) - 1)
    def _():
        row0 = jnp.sum(acc[0], axis=0, keepdims=True)
        row1 = jnp.sum(acc[1], axis=0, keepdims=True)
        one = lax.broadcasted_iota(jnp.int32, (1, 128), 1)
        sq_ref[...] = jnp.concatenate(
            [row0, jnp.where(one == 0, row1, later_ref[:, :128]), later_ref[:, 128:]], axis=1)


def sf_spec(c):
    return pl.BlockSpec((3, 3, c), lambda i: (0, 0, i))


def tail(docs, base, gate, key, value, sf):
    ch, n = gate.shape
    c = min(BL, ch)
    wide = pl.BlockSpec((c, 256), lambda i: (i, n // 256 - 1))
    return pl.pallas_call(
        tail_kernel, grid=(ch // c,),
        in_specs=[SMEM, SMEM, wide, wide, wide, sf_spec(c)],
        out_specs=pl.BlockSpec((c // CB, ENDS, 128), lambda i: (i, 0, 0)),
        out_shape=jax.ShapeDtypeStruct((ch // CB, ENDS, 128), BF),
        scratch_shapes=[pltpu.VMEM((2, GROUP, 128), BF)],
        compiler_params=pltpu.CompilerParams(vmem_limit_bytes=BIG), name="tail",
    )(docs, base, gate, key, value, sf)


def param_specs(c):
    row = pl.BlockSpec((1, c), lambda i: (0, i))
    return [sf_spec(c), row, pl.BlockSpec((c // GROUP, MR), lambda i: (i, 0))]


def later(docs, base, gate, key, value, sf, skip, taps):
    ch, n = gate.shape
    c = min(BL, ch)
    wide = pl.BlockSpec((c, n), lambda i: (i, 0))
    tile = pl.BlockSpec((c, 128), lambda i: (i, 0))
    return pl.pallas_call(
        later_kernel, grid=(ch // c,),
        in_specs=[SMEM, SMEM, wide, wide, wide] + param_specs(c),
        out_specs=[wide, tile, tile, pl.BlockSpec((c // CB, 16, CB), lambda i: (i, 0, 0)),
                   pl.BlockSpec((c // GROUP, MR, MR), lambda i: (i, 0, 0)), pl.BlockSpec((1, n - 128), lambda i: (0, 0))],
        out_shape=[jax.ShapeDtypeStruct((ch, n), BF), jax.ShapeDtypeStruct((ch, 128), F32),
                   jax.ShapeDtypeStruct((ch, 128), BF), jax.ShapeDtypeStruct((ch // CB, 16, CB), BF),
                   jax.ShapeDtypeStruct((ch // GROUP, MR, MR), BF), jax.ShapeDtypeStruct((1, n - 128), F32)],
        scratch_shapes=[pltpu.VMEM((3, 256, 128), BF), pltpu.VMEM((2, GROUP, n), BF), pltpu.VMEM((GROUP, 128), BF),
                        pltpu.VMEM((8, n - 128), F32)],
        cost_estimate=pl.CostEstimate(flops=2 * ch * 384 * 256 * 8, bytes_accessed=8 * ch * n, transcendentals=0),
        compiler_params=pltpu.CompilerParams(vmem_limit_bytes=BIG), name="later",
    )(docs, base, gate, key, value, sf, skip, taps)


def first(docs, base, halo, done, sf, skip, taps):
    done = [pltpu.with_memory_space_constraint(x, pltpu.HBM) for x in done]
    rows, aux, prod, own, rings, squares = done
    ch, n = rows.shape
    c = min(BL, ch)
    half = pl.BlockSpec((c, 256), lambda i: (i, 0))
    tile = pl.BlockSpec((c, 128), lambda i: (i, 0))
    whole = lambda w: pl.BlockSpec((1, w), lambda i: (0, 0))
    return pl.pallas_call(
        first_kernel, grid=(ch // c,),
        in_specs=[SMEM, SMEM, pl.BlockSpec((c // CB, ENDS, 128), lambda i: (i, 0, 0)), half, tile, tile,
                  pl.BlockSpec((c // CB, 16, CB), lambda i: (i, 0, 0)),
                  pl.BlockSpec((c // GROUP, MR, MR), lambda i: (i, 0, 0)), whole(n - 128)] + param_specs(c),
        out_specs=[half, whole(n)],
        out_shape=[jax.ShapeDtypeStruct((ch, n), BF), jax.ShapeDtypeStruct((1, n), F32)],
        scratch_shapes=[pltpu.VMEM((256, 128), BF), pltpu.VMEM((8, 128), F32), pltpu.VMEM((2, 8, 128), F32)],
        input_output_aliases={3: 0},
        cost_estimate=pl.CostEstimate(flops=2 * ch * 128 * 256 * 8, bytes_accessed=4 * ch * n, transcendentals=0),
        compiler_params=pltpu.CompilerParams(vmem_limit_bytes=FIRST_VMEM), name="first",
    )(docs, base, halo, rows, aux, prod, own, rings, squares, sf, skip, taps)


FIRST_VMEM = 24 << 20
def final_kernel(recv_ref, sums_ref, gain_ref, out_ref):
    per, c, n = recv_ref.shape
    gain = jnp.broadcast_to(gain_ref[...], (c, n))
    for i in range(per):
        scale = lax.rsqrt(sums_ref[i] / D + EPS)
        out_ref[:, n * i:n * (i + 1)] = (recv_ref[i].astype(F32) * scale * gain).astype(BF)


def final(recv, sums, gain):
    k, c, n = recv.shape
    per = min(k, PER)
    return pl.pallas_call(
        final_kernel, grid=(k // per,),
        in_specs=[pl.BlockSpec((per, c, n), lambda i: (i, 0, 0)), pl.BlockSpec((per, 1, n), lambda i: (i, 0, 0)),
                  pl.BlockSpec((c, 1), lambda i: (0, 0))],
        out_specs=pl.BlockSpec((c, per * n), lambda i: (0, i)),
        out_shape=jax.ShapeDtypeStruct((c, k * n), BF),
        compiler_params=pltpu.CompilerParams(vmem_limit_bytes=24 << 20), name="settle",
    )(recv, sums, gain)


ROUNDS = (((0, 1), (2, 3), (4, 5), (6, 7)), ((1, 2), (3, 4), (5, 6), (7, 0)), ((0, 3), (7, 4), (1, 6), (2, 5)))


def channel_sum(x):
    if lax.axis_size("ch") != 8:
        return lax.psum(x, "ch"), jnp.zeros_like(x)
    for pairs in ROUNDS[:-1]:
        x = x + lax.ppermute(x, "ch", list(pairs) + [(b, a) for a, b in pairs])
    return x, lax.ppermute(x, "ch", list(ROUNDS[-1]) + [(b, a) for a, b in ROUNDS[-1]])


def local(gate, key, value, sf, taps, skip, gain, docs):
    place = lax.axis_index("ctx")
    width = lax.axis_size("ctx")
    ch, n = gate.shape
    base = (place * n).astype(jnp.int32).reshape(1)
    skip = skip.reshape(1, ch)
    gain = lax.dynamic_slice_in_dim(gain, place * (ch // width), ch // width).reshape(ch // width, 1)
    ends = tail(docs, base, gate, key, value, sf)
    halo = lax.ppermute(ends, "ctx", [(i, i + 1) for i in range(width - 1)])
    done = later(docs, base, gate, key, value, sf, skip, taps)
    rows, squares = first(docs, base, halo, done, sf, skip, taps)
    recv = lax.all_to_all(rows.reshape(width, ch // width, n), "ctx", split_axis=0, concat_axis=0, tiled=True)
    near, far = channel_sum(squares)
    far, recv = lax.optimization_barrier((far, recv))
    sums = lax.all_to_all(jnp.broadcast_to((near + far)[None], (width, 1, n)), "ctx", split_axis=0, concat_axis=0, tiled=True)
    return final(recv, sums, gain)


def solution(mesh):
    in_specs = (P("ch", "ctx"),) * 3 + (P(None, None, "ch"), P("ch", None), P("ch"), P("ch"), P())
    return jax.shard_map(local, mesh=mesh, in_specs=in_specs, out_specs=P(("ch", "ctx"), None), check_vma=False)
```

```python
import jax
import jax.numpy as jnp
from jax import lax
from jax.experimental import pallas as pl
from jax.experimental.pallas import tpu as pltpu
from jax.sharding import PartitionSpec as P

D = 8192
GROUP = 16
MR = 128
EPS = 1e-6
DOCS = 64
F32 = jnp.float32
BF = jnp.bfloat16
CB = 128
BL = 512
ENDS = 144
PER = 16
BIG = 56 << 20
SMEM = pl.BlockSpec(memory_space=pltpu.SMEM)


def starts_row(docs_ref, base, count):
    pos = lax.broadcasted_iota(jnp.int32, (1, count), 1) + base
    first = jnp.int32(0)
    start = jnp.zeros((1, count), jnp.int32)
    for d in range(DOCS):
        start = jnp.where(pos >= first, first, start)
        first = first + docs_ref[d]
    return pos, start


def as_bf(flag, shape):
    return jnp.broadcast_to(flag.astype(F32), shape).astype(BF)


def tile_masks(first):
    s = lax.broadcasted_iota(jnp.int32, (128, 128), 0)
    t = lax.broadcasted_iota(jnp.int32, (128, 128), 1)
    return (((s > t) & (s - 128 >= first)).astype(F32).astype(BF), ((s <= t) & (s >= first)).astype(F32).astype(BF))


def spread(rows):
    count = sum(r.shape[0] for r in rows)
    rest = jnp.concatenate(rows + [jnp.zeros((16 - count, CB), F32)], axis=0)
    pieces = []
    for _ in range(3):
        pieces.append(rest.astype(BF))
        rest = rest - pieces[-1].astype(F32)
    row = lax.broadcasted_iota(jnp.int32, (16, 128 * count), 0)
    column = lax.broadcasted_iota(jnp.int32, (16, 128 * count), 1)
    ones = ((column >= 128 * row) & (column < 128 * row + 128)).astype(F32).astype(BF)
    return lax.dot_general(jnp.concatenate(pieces, axis=0), jnp.concatenate([ones] * 3, axis=0),
                           (((0,), (0,)), ((), ())), preferred_element_type=F32)


def lanes_of(wide, i, tiles=1):
    part = wide[:, 128 * i:128 * (i + 1)]
    return part if tiles == 1 else jnp.concatenate([part] * tiles, axis=1)


def conv3(raw, keeps, cols, first):
    one = pltpu.roll(raw, 1, 1) * keeps[0]
    two = pltpu.roll(raw, 2, 1) * keeps[1]
    k = raw.shape[1] // 128
    return (lanes_of(cols, first, k) * raw.astype(F32) + lanes_of(cols, first + 1, k) * one.astype(F32)
            + lanes_of(cols, first + 2, k) * two.astype(F32))


def ring_of(taps):
    return pltpu.roll(jnp.broadcast_to(taps, (128, 128)), 0, 1, stride=1, stride_axis=0).astype(BF)


def pick(here, *wanted):
    row = lax.broadcasted_iota(jnp.int32, (16, 128), 0)
    lane = lax.broadcasted_iota(jnp.int32, (16, 128), 1)
    out = jnp.zeros((16, CB), F32)
    for ref, lanes, at, first, count in wanted:
        one_hot = ((lane - first == row - at) & (row >= at) & (row < at + count)).astype(F32).astype(BF)
        out = out + lax.dot_general(one_hot, ref[here, lanes], (((1,), (1,)), ((), ())), preferred_element_type=F32)
    return out.astype(BF)


def tail_kernel(docs_ref, base_ref, gate_ref, key_ref, value_ref, sf_ref, out_ref, keeps):
    @pl.when(pl.program_id(0) == 0)
    def _():
        pos, start = starts_row(docs_ref, base_ref[0] + 384, 128)
        for lag in (1, 2):
            keeps[lag - 1] = as_bf(pos - lag >= start, (GROUP, 128))

    last = lax.broadcasted_iota(jnp.int32, (GROUP, 128), 1) == 127

    def filtered(ref, at, cols, i):
        raw = ref[at, 128:]
        one = pltpu.roll(raw, 1, 1) * keeps[0]
        two = pltpu.roll(jnp.where(last, ref[at, :128], raw), 2, 1) * keeps[1]
        return (lanes_of(cols, i) * raw.astype(F32) + lanes_of(cols, i + 1) * one.astype(F32)
                + lanes_of(cols, i + 2) * two.astype(F32))

    for b in range(gate_ref.shape[0] // CB):
        here = slice(CB * b, CB * (b + 1))
        sf = sf_ref[:, :, here]
        cols = spread([sf[1], sf[2]])
        for g in range(CB // GROUP):
            at = slice(CB * b + GROUP * g, CB * b + GROUP * (g + 1))
            c = cols[GROUP * g:GROUP * (g + 1)]
            out_ref[b, GROUP * g:GROUP * (g + 1)] = (filtered(key_ref, at, c, 0) * filtered(value_ref, at, c, 3)).astype(BF)
        lanes = slice(128, 256)
        out_ref[b, CB:] = pick(here, (gate_ref, lanes, 0, 126, 2), (key_ref, lanes, 2, 126, 2), (value_ref, lanes, 4, 126, 2))


def later_kernel(docs_ref, base_ref, gate_ref, key_ref, value_ref, sf_ref, skip_ref, taps_ref,
                 out_ref, aux_ref, prod_ref, own_ref, ring_ref, sq_ref, masks, keeps, inner, acc):
    step = pl.program_id(0)

    @pl.when(step == 0)
    def _():
        pos, start = starts_row(docs_ref, base_ref[0], 512)
        rel = pos - base_ref[0]
        for lag in (1, 2):
            keeps[lag - 1] = as_bf((pos - lag >= start) & (rel >= lag), (GROUP, 512))
        inner[...] = as_bf(rel[:, :128] >= 2, (GROUP, 128))
        for j in range(3):
            first = start[:, 128 * (j + 1):128 * (j + 2)] - (base_ref[0] + 128 * (j + 1))
            masks[j, :128, :], masks[j, 128:, :] = tile_masks(jnp.broadcast_to(first, (128, 128)))
        acc[...] = jnp.zeros_like(acc)

    total = acc[...]
    for b in range(gate_ref.shape[0] // CB):
        here = slice(CB * b, CB * (b + 1))
        sf = sf_ref[:, :, here]
        cols = spread([sf[0], sf[1], sf[2], skip_ref[:, here]])
        taps = taps_ref[8 * b:8 * (b + 1)].astype(BF).astype(F32)
        for g in range(CB // GROUP):
            at = slice(CB * b + GROUP * g, CB * b + GROUP * (g + 1))
            c = cols[GROUP * g:GROUP * (g + 1)]
            product = (conv3(key_ref[at], keeps, c, 3) * conv3(value_ref[at], keeps, c, 6)).astype(BF)
            product = jnp.concatenate([product[:, :128] * inner[...], product[:, 128:]], axis=1)
            prod_ref[at] = product[:, :128]
            gate = conv3(gate_ref[at], keeps, c, 0)
            ring = ring_of(taps[g:g + 1])
            ring_ref[8 * b + g] = ring
            both = jnp.concatenate([ring, ring], axis=0)
            mixed = jnp.concatenate([
                jnp.dot(product[:, 128 * j:128 * j + 256], both * masks[j], preferred_element_type=F32)
                for j in range(3)], axis=1)
            mixed = mixed + lanes_of(c, 9, 3) * product[:, 128:].astype(F32)
            gated = gate[:, 128:] * mixed
            aux_ref[at] = gate[:, :128]
            square = gated * gated
            total = total + square[:8] + square[8:]
            out_ref[at, 128:] = gated.astype(BF)
            out_ref[at, :128] = jnp.zeros((GROUP, 128), BF)
        tile0, tile1 = slice(0, 128), slice(128, 256)
        own_ref[b] = pick(here, (gate_ref, tile0, 0, 0, 2), (key_ref, tile0, 2, 0, 2), (value_ref, tile0, 4, 0, 2),
                          (gate_ref, tile0, 6, 126, 2), (gate_ref, tile1, 8, 0, 1))
    acc[...] = total

    @pl.when(step == pl.num_programs(0) - 1)
    def _():
        sq_ref[...] = jnp.sum(acc[...], axis=0, keepdims=True)


def first_kernel(docs_ref, base_ref, halo_ref, rows_ref, aux_ref, prod_ref, own_ref, ring_ref, later_ref, sf_ref, skip_ref,
                 taps_ref, out_ref, sq_ref, masks, keeps, acc):
    step = pl.program_id(0)

    @pl.when(step == 0)
    def _():
        pos, start = starts_row(docs_ref, base_ref[0], 256)
        for lag in (1, 2):
            keeps[lag - 1:lag] = (pos[:, :128] - lag >= start[:, :128]).astype(F32)
        for lag in (1, 2, 127):
            row = 1 + lag if lag < 3 else 4
            keeps[row:row + 1] = (pos[:, 128:] - lag >= start[:, 128:]).astype(F32)
        masks[:128], masks[128:] = tile_masks(jnp.broadcast_to(start[:, :128] - base_ref[0], (128, 128)))
        acc[...] = jnp.zeros_like(acc)

    lane = lax.broadcasted_iota(jnp.int32, (GROUP, 128), 1)
    one_hot = (lax.broadcasted_iota(jnp.int32, (16, 128), 0) == lane).astype(F32).astype(BF)
    total0, total1 = acc[0], acc[1]
    for b in range(halo_ref.shape[0]):
        here = slice(CB * b, CB * (b + 1))
        own = own_ref[b].astype(F32)
        past = halo_ref[b, CB:].astype(F32)

        def both_positions(i):
            t = [sf_ref[i, lag:lag + 1, here] for lag in range(3)]
            x = own[2 * i:2 * i + 2]
            h = past[2 * i:2 * i + 2]
            at0 = t[0] * x[:1] + keeps[0:1, 0:1] * (t[1] * h[1:]) + keeps[1:2, 0:1] * (t[2] * h[:1])
            at1 = t[0] * x[1:] + keeps[0:1, 1:2] * (t[1] * x[:1]) + keeps[1:2, 1:2] * (t[2] * h[1:])
            return jnp.concatenate([at0, at1], axis=0)

        two = (both_positions(1) * both_positions(2)).astype(BF).astype(F32)
        t = [sf_ref[0, lag:lag + 1, here] for lag in range(3)]
        gate = t[0] * own[8:9] + keeps[2:3, 0:1] * (t[1] * own[7:8]) + keeps[3:4, 0:1] * (t[2] * own[6:7])
        cols = spread([skip_ref[:, here], both_positions(0), keeps[4:5, 0:1] * two[1:] * gate])
        put = lax.dot_general(jnp.concatenate([two, jnp.zeros((14, CB), F32)], axis=0).astype(BF), one_hot,
                              (((0,), (0,)), ((), ())), preferred_element_type=F32)
        taps = taps_ref[8 * b:8 * (b + 1)].astype(BF).astype(F32)
        for g in range(CB // GROUP):
            at = slice(CB * b + GROUP * g, CB * b + GROUP * (g + 1))
            inside = slice(GROUP * g, GROUP * (g + 1))
            c = cols[inside]
            product = prod_ref[at] + put[inside].astype(BF)
            ring = ring_ref[8 * b + g]
            mixed = jnp.dot(jnp.concatenate([halo_ref[b, inside], product], axis=1),
                            jnp.concatenate([ring, ring], axis=0) * masks[...], preferred_element_type=F32)
            mixed = mixed + lanes_of(c, 0) * product.astype(F32)
            gated = jnp.where(lane == 0, lanes_of(c, 1), jnp.where(lane == 1, lanes_of(c, 2), aux_ref[at])) * mixed
            old = rows_ref[at, 128:].astype(F32)
            after = jnp.where(lane == 0, old + lanes_of(c, 3) * taps[g:g + 1, 127:128], old)
            square = gated * gated
            total0 = total0 + square[:8] + square[8:]
            square = after * after
            total1 = total1 + square[:8] + square[8:]
            out_ref[at, :128] = gated.astype(BF)
            out_ref[at, 128:] = after.astype(BF)
    acc[0], acc[1] = total0, total1

    @pl.when(step == pl.num_programs(0) - 1)
    def _():
        row0 = jnp.sum(acc[0], axis=0, keepdims=True)
        row1 = jnp.sum(acc[1], axis=0, keepdims=True)
        one = lax.broadcasted_iota(jnp.int32, (1, 128), 1)
        sq_ref[...] = jnp.concatenate(
            [row0, jnp.where(one == 0, row1, later_ref[:, :128]), later_ref[:, 128:]], axis=1)


def sf_spec(c):
    return pl.BlockSpec((3, 3, c), lambda i: (0, 0, i))


def tail(docs, base, gate, key, value, sf):
    ch, n = gate.shape
    c = min(BL, ch)
    wide = pl.BlockSpec((c, 256), lambda i: (i, n // 256 - 1))
    return pl.pallas_call(
        tail_kernel, grid=(ch // c,),
        in_specs=[SMEM, SMEM, wide, wide, wide, sf_spec(c)],
        out_specs=pl.BlockSpec((c // CB, ENDS, 128), lambda i: (i, 0, 0)),
        out_shape=jax.ShapeDtypeStruct((ch // CB, ENDS, 128), BF),
        scratch_shapes=[pltpu.VMEM((2, GROUP, 128), BF)],
        compiler_params=pltpu.CompilerParams(vmem_limit_bytes=LATER_VMEM), name="tail",
    )(docs, base, gate, key, value, sf)


def param_specs(c):
    row = pl.BlockSpec((1, c), lambda i: (0, i))
    return [sf_spec(c), row, pl.BlockSpec((c // GROUP, MR), lambda i: (i, 0))]


def later(docs, base, gate, key, value, sf, skip, taps):
    ch, n = gate.shape
    c = min(BL, ch)
    wide = pl.BlockSpec((c, n), lambda i: (i, 0))
    tile = pl.BlockSpec((c, 128), lambda i: (i, 0))
    return pl.pallas_call(
        later_kernel, grid=(ch // c,),
        in_specs=[SMEM, SMEM, wide, wide, wide] + param_specs(c),
        out_specs=[wide, tile, tile, pl.BlockSpec((c // CB, 16, CB), lambda i: (i, 0, 0)),
                   pl.BlockSpec((c // GROUP, MR, MR), lambda i: (i, 0, 0)), pl.BlockSpec((1, n - 128), lambda i: (0, 0))],
        out_shape=[pltpu.HBM((ch, n), BF), jax.ShapeDtypeStruct((ch, 128), F32),
                   jax.ShapeDtypeStruct((ch, 128), BF), jax.ShapeDtypeStruct((ch // CB, 16, CB), BF),
                   jax.ShapeDtypeStruct((ch // GROUP, MR, MR), BF), jax.ShapeDtypeStruct((1, n - 128), F32)],
        scratch_shapes=[pltpu.VMEM((3, 256, 128), BF), pltpu.VMEM((2, GROUP, n), BF), pltpu.VMEM((GROUP, 128), BF),
                        pltpu.VMEM((8, n - 128), F32)],
        cost_estimate=pl.CostEstimate(flops=2 * ch * 384 * 256 * 8, bytes_accessed=8 * ch * n, transcendentals=0),
        compiler_params=pltpu.CompilerParams(vmem_limit_bytes=LATER_VMEM), name="later",
    )(docs, base, gate, key, value, sf, skip, taps)


def first(docs, base, halo, done, sf, skip, taps):
    done = [pltpu.with_memory_space_constraint(x, pltpu.HBM if i == 0 else pltpu.VMEM) for i, x in enumerate(done)]
    rows, aux, prod, own, rings, squares = done
    ch, n = rows.shape
    c = min(BL, ch)
    half = pl.BlockSpec((c, 256), lambda i: (i, 0))
    tile = pl.BlockSpec((c, 128), lambda i: (i, 0))
    whole = lambda w: pl.BlockSpec((1, w), lambda i: (0, 0))
    return pl.pallas_call(
        first_kernel, grid=(ch // c,),
        in_specs=[SMEM, SMEM, pl.BlockSpec((c // CB, ENDS, 128), lambda i: (i, 0, 0)), half, tile, tile,
                  pl.BlockSpec((c // CB, 16, CB), lambda i: (i, 0, 0)),
                  pl.BlockSpec((c // GROUP, MR, MR), lambda i: (i, 0, 0)), whole(n - 128)] + param_specs(c),
        out_specs=[half, whole(n)],
        out_shape=[jax.ShapeDtypeStruct((ch, n), BF), jax.ShapeDtypeStruct((1, n), F32)],
        scratch_shapes=[pltpu.VMEM((256, 128), BF), pltpu.VMEM((8, 128), F32), pltpu.VMEM((2, 8, 128), F32)],
        input_output_aliases={3: 0},
        cost_estimate=pl.CostEstimate(flops=2 * ch * 128 * 256 * 8, bytes_accessed=4 * ch * n, transcendentals=0),
        compiler_params=pltpu.CompilerParams(vmem_limit_bytes=FIRST_VMEM), name="first",
    )(docs, base, halo, rows, aux, prod, own, rings, squares, sf, skip, taps)


FIRST_VMEM = 24 << 20
LATER_VMEM = 40 << 20
def final_kernel(recv_ref, sums_ref, gain_ref, out_ref):
    per, c, n = recv_ref.shape
    gain = jnp.broadcast_to(gain_ref[...], (c, n))
    for i in range(per):
        scale = lax.rsqrt(sums_ref[i] / D + EPS)
        out_ref[:, n * i:n * (i + 1)] = (recv_ref[i].astype(F32) * scale * gain).astype(BF)


def final(recv, sums, gain):
    k, c, n = recv.shape
    per = min(k, PER)
    return pl.pallas_call(
        final_kernel, grid=(k // per,),
        in_specs=[pl.BlockSpec((per, c, n), lambda i: (i, 0, 0)), pl.BlockSpec((per, 1, n), lambda i: (i, 0, 0)),
                  pl.BlockSpec((c, 1), lambda i: (0, 0))],
        out_specs=pl.BlockSpec((c, per * n), lambda i: (0, i)),
        out_shape=jax.ShapeDtypeStruct((c, k * n), BF),
        compiler_params=pltpu.CompilerParams(vmem_limit_bytes=24 << 20), name="settle",
    )(recv, sums, gain)


ROUNDS = (((0, 1), (2, 3), (4, 5), (6, 7)), ((1, 2), (3, 4), (5, 6), (7, 0)), ((0, 3), (7, 4), (1, 6), (2, 5)))


def channel_sum(x):
    if lax.axis_size("ch") != 8:
        return lax.psum(x, "ch"), jnp.zeros_like(x)
    for pairs in ROUNDS[:-1]:
        x = x + lax.ppermute(x, "ch", list(pairs) + [(b, a) for a, b in pairs])
    return x, lax.ppermute(x, "ch", list(ROUNDS[-1]) + [(b, a) for a, b in ROUNDS[-1]])


def local(gate, key, value, sf, taps, skip, gain, docs):
    place = lax.axis_index("ctx")
    width = lax.axis_size("ctx")
    ch, n = gate.shape
    base = (place * n).astype(jnp.int32).reshape(1)
    skip = skip.reshape(1, ch)
    gain = lax.dynamic_slice_in_dim(gain, place * (ch // width), ch // width).reshape(ch // width, 1)
    gate, key, value = (pltpu.with_memory_space_constraint(x, pltpu.HBM) for x in (gate, key, value))
    ends = tail(pltpu.with_memory_space_constraint(docs, pltpu.HBM), base, gate, key, value, pltpu.with_memory_space_constraint(sf, pltpu.HBM))
    halo = lax.ppermute(ends, "ctx", [(i, i + 1) for i in range(width - 1)])
    done = later(docs, base, gate, key, value, sf, skip, taps)
    rows, squares = first(docs, base, halo, done, sf, skip, taps)
    recv = lax.all_to_all(rows.reshape(width, ch // width, n), "ctx", split_axis=0, concat_axis=0, tiled=True)
    near, far = channel_sum(squares)
    far, recv = lax.optimization_barrier((far, recv))
    sums = lax.all_to_all(jnp.broadcast_to((near + far)[None], (width, 1, n)), "ctx", split_axis=0, concat_axis=0, tiled=True)
    return final(recv, sums, gain)


def solution(mesh):
    in_specs = (P("ch", "ctx"),) * 3 + (P(None, None, "ch"), P("ch", None), P("ch"), P("ch"), P())
    return jax.shard_map(local, mesh=mesh, in_specs=in_specs, out_specs=P(("ch", "ctx"), None), check_vma=False)
```

```python
import jax
import jax.numpy as jnp
from jax import lax
from jax.experimental import pallas as pl
from jax.experimental.pallas import tpu as pltpu
from jax.sharding import PartitionSpec as P

D = 8192
GROUP = 16
MR = 128
EPS = 1e-6
DOCS = 64
F32 = jnp.float32
BF = jnp.bfloat16
CB = 128
BL = 512
ENDS = 144
PER = 16
BIG = 56 << 20
SMEM = pl.BlockSpec(memory_space=pltpu.SMEM)


def starts_row(docs_ref, base, count):
    pos = lax.broadcasted_iota(jnp.int32, (1, count), 1) + base
    first = jnp.int32(0)
    start = jnp.zeros((1, count), jnp.int32)
    for d in range(DOCS):
        start = jnp.where(pos >= first, first, start)
        first = first + docs_ref[d]
    return pos, start


def as_bf(flag, shape):
    return jnp.broadcast_to(flag.astype(F32), shape).astype(BF)


def tile_masks(first):
    s = lax.broadcasted_iota(jnp.int32, (128, 128), 0)
    t = lax.broadcasted_iota(jnp.int32, (128, 128), 1)
    return (((s > t) & (s - 128 >= first)).astype(F32).astype(BF), ((s <= t) & (s >= first)).astype(F32).astype(BF))


def spread(rows):
    count = sum(r.shape[0] for r in rows)
    rest = jnp.concatenate(rows + [jnp.zeros((16 - count, CB), F32)], axis=0)
    pieces = []
    for _ in range(3):
        pieces.append(rest.astype(BF))
        rest = rest - pieces[-1].astype(F32)
    row = lax.broadcasted_iota(jnp.int32, (16, 128 * count), 0)
    column = lax.broadcasted_iota(jnp.int32, (16, 128 * count), 1)
    ones = ((column >= 128 * row) & (column < 128 * row + 128)).astype(F32).astype(BF)
    return lax.dot_general(jnp.concatenate(pieces, axis=0), jnp.concatenate([ones] * 3, axis=0),
                           (((0,), (0,)), ((), ())), preferred_element_type=F32)


def lanes_of(wide, i, tiles=1):
    part = wide[:, 128 * i:128 * (i + 1)]
    return part if tiles == 1 else jnp.concatenate([part] * tiles, axis=1)


def conv3(raw, keeps, cols, first):
    one = pltpu.roll(raw, 1, 1) * keeps[0]
    two = pltpu.roll(raw, 2, 1) * keeps[1]
    k = raw.shape[1] // 128
    return (lanes_of(cols, first, k) * raw.astype(F32) + lanes_of(cols, first + 1, k) * one.astype(F32)
            + lanes_of(cols, first + 2, k) * two.astype(F32))


def ring_of(taps):
    return pltpu.roll(jnp.broadcast_to(taps, (128, 128)), 0, 1, stride=1, stride_axis=0).astype(BF)


def pick(here, *wanted):
    row = lax.broadcasted_iota(jnp.int32, (16, 128), 0)
    lane = lax.broadcasted_iota(jnp.int32, (16, 128), 1)
    out = jnp.zeros((16, CB), F32)
    for ref, lanes, at, first, count in wanted:
        one_hot = ((lane - first == row - at) & (row >= at) & (row < at + count)).astype(F32).astype(BF)
        out = out + lax.dot_general(one_hot, ref[here, lanes], (((1,), (1,)), ((), ())), preferred_element_type=F32)
    return out.astype(BF)


def tail_kernel(docs_ref, base_ref, gate_ref, key_ref, value_ref, sf_ref, out_ref, keeps):
    @pl.when(pl.program_id(0) == 0)
    def _():
        pos, start = starts_row(docs_ref, base_ref[0] + 384, 128)
        for lag in (1, 2):
            keeps[lag - 1] = as_bf(pos - lag >= start, (GROUP, 128))

    last = lax.broadcasted_iota(jnp.int32, (GROUP, 128), 1) == 127

    def filtered(ref, at, cols, i):
        raw = ref[at, 128:]
        one = pltpu.roll(raw, 1, 1) * keeps[0]
        two = pltpu.roll(jnp.where(last, ref[at, :128], raw), 2, 1) * keeps[1]
        return (lanes_of(cols, i) * raw.astype(F32) + lanes_of(cols, i + 1) * one.astype(F32)
                + lanes_of(cols, i + 2) * two.astype(F32))

    for b in range(gate_ref.shape[0] // CB):
        here = slice(CB * b, CB * (b + 1))
        sf = sf_ref[:, :, here]
        cols = spread([sf[1], sf[2]])
        for g in range(CB // GROUP):
            at = slice(CB * b + GROUP * g, CB * b + GROUP * (g + 1))
            c = cols[GROUP * g:GROUP * (g + 1)]
            out_ref[b, GROUP * g:GROUP * (g + 1)] = (filtered(key_ref, at, c, 0) * filtered(value_ref, at, c, 3)).astype(BF)
        lanes = slice(128, 256)
        out_ref[b, CB:] = pick(here, (gate_ref, lanes, 0, 126, 2), (key_ref, lanes, 2, 126, 2), (value_ref, lanes, 4, 126, 2))


def later_kernel(docs_ref, base_ref, gate_ref, key_ref, value_ref, sf_ref, skip_ref, taps_ref,
                 out_ref, aux_ref, prod_ref, own_ref, ring_ref, sq_ref, masks, keeps, inner, acc):
    step = pl.program_id(0)

    @pl.when(step == 0)
    def _():
        pos, start = starts_row(docs_ref, base_ref[0], 512)
        rel = pos - base_ref[0]
        for lag in (1, 2):
            keeps[lag - 1] = as_bf((pos - lag >= start) & (rel >= lag), (GROUP, 512))
        inner[...] = as_bf(rel[:, :128] >= 2, (GROUP, 128))
        for j in range(3):
            first = start[:, 128 * (j + 1):128 * (j + 2)] - (base_ref[0] + 128 * (j + 1))
            masks[j, :128, :], masks[j, 128:, :] = tile_masks(jnp.broadcast_to(first, (128, 128)))
        acc[...] = jnp.zeros_like(acc)

    total = acc[...]
    for b in range(gate_ref.shape[0] // CB):
        here = slice(CB * b, CB * (b + 1))
        sf = sf_ref[:, :, here]
        cols = spread([sf[0], sf[1], sf[2], skip_ref[:, here]])
        taps = taps_ref[8 * b:8 * (b + 1)].astype(BF).astype(F32)
        for g in range(CB // GROUP):
            at = slice(CB * b + GROUP * g, CB * b + GROUP * (g + 1))
            c = cols[GROUP * g:GROUP * (g + 1)]
            product = (conv3(key_ref[at], keeps, c, 3) * conv3(value_ref[at], keeps, c, 6)).astype(BF)
            product = jnp.concatenate([product[:, :128] * inner[...], product[:, 128:]], axis=1)
            prod_ref[at] = product[:, :128]
            gate = conv3(gate_ref[at], keeps, c, 0)
            ring = ring_of(taps[g:g + 1])
            ring_ref[8 * b + g] = ring
            both = jnp.concatenate([ring, ring], axis=0)
            mixed = jnp.concatenate([
                jnp.dot(product[:, 128 * j:128 * j + 256], both * masks[j], preferred_element_type=F32)
                for j in range(3)], axis=1)
            mixed = mixed + lanes_of(c, 9, 3) * product[:, 128:].astype(F32)
            gated = gate[:, 128:] * mixed
            aux_ref[at] = gate[:, :128]
            square = gated * gated
            total = total + square[:8] + square[8:]
            out_ref[at, 128:] = gated.astype(BF)
            out_ref[at, :128] = jnp.zeros((GROUP, 128), BF)
        tile0, tile1 = slice(0, 128), slice(128, 256)
        own_ref[b] = pick(here, (gate_ref, tile0, 0, 0, 2), (key_ref, tile0, 2, 0, 2), (value_ref, tile0, 4, 0, 2),
                          (gate_ref, tile0, 6, 126, 2), (gate_ref, tile1, 8, 0, 1))
    acc[...] = total

    @pl.when(step == pl.num_programs(0) - 1)
    def _():
        sq_ref[...] = jnp.sum(acc[...], axis=0, keepdims=True)


def first_kernel(docs_ref, base_ref, halo_ref, rows_ref, aux_ref, prod_ref, own_ref, ring_ref, later_ref, sf_ref, skip_ref,
                 taps_ref, out_ref, sq_ref, masks, keeps, acc):
    step = pl.program_id(0)

    @pl.when(step == 0)
    def _():
        pos, start = starts_row(docs_ref, base_ref[0], 256)
        for lag in (1, 2):
            keeps[lag - 1:lag] = (pos[:, :128] - lag >= start[:, :128]).astype(F32)
        for lag in (1, 2, 127):
            row = 1 + lag if lag < 3 else 4
            keeps[row:row + 1] = (pos[:, 128:] - lag >= start[:, 128:]).astype(F32)
        masks[:128], masks[128:] = tile_masks(jnp.broadcast_to(start[:, :128] - base_ref[0], (128, 128)))
        acc[...] = jnp.zeros_like(acc)

    lane = lax.broadcasted_iota(jnp.int32, (GROUP, 128), 1)
    total0, total1 = acc[0], acc[1]
    for b in range(halo_ref.shape[0]):
        here = slice(CB * b, CB * (b + 1))
        own = own_ref[b].astype(F32)
        past = halo_ref[b, CB:].astype(F32)

        def both_positions(i):
            t = [sf_ref[i, lag:lag + 1, here] for lag in range(3)]
            x = own[2 * i:2 * i + 2]
            h = past[2 * i:2 * i + 2]
            at0 = t[0] * x[:1] + keeps[0:1, 0:1] * (t[1] * h[1:]) + keeps[1:2, 0:1] * (t[2] * h[:1])
            at1 = t[0] * x[1:] + keeps[0:1, 1:2] * (t[1] * x[:1]) + keeps[1:2, 1:2] * (t[2] * h[1:])
            return jnp.concatenate([at0, at1], axis=0)

        two = (both_positions(1) * both_positions(2)).astype(BF).astype(F32)
        t = [sf_ref[0, lag:lag + 1, here] for lag in range(3)]
        gate = t[0] * own[8:9] + keeps[2:3, 0:1] * (t[1] * own[7:8]) + keeps[3:4, 0:1] * (t[2] * own[6:7])
        cols = spread([skip_ref[:, here], both_positions(0), keeps[4:5, 0:1] * two[1:] * gate, two])
        taps = taps_ref[8 * b:8 * (b + 1)].astype(BF).astype(F32)
        for g in range(CB // GROUP):
            at = slice(CB * b + GROUP * g, CB * b + GROUP * (g + 1))
            inside = slice(GROUP * g, GROUP * (g + 1))
            c = cols[inside]
            product = prod_ref[at]
            ring = ring_ref[8 * b + g]
            mixed = jnp.dot(jnp.concatenate([halo_ref[b, inside], product], axis=1),
                            jnp.concatenate([ring, ring], axis=0) * masks[...], preferred_element_type=F32)
            skip = lanes_of(c, 0)
            near = ring[:16].astype(F32) * masks[128:144].astype(F32)
            mixed = (mixed + skip * product.astype(F32)
                     + lanes_of(c, 4) * (near[0:1] + jnp.where(lane == 0, skip, 0.0))
                     + lanes_of(c, 5) * (near[1:2] + jnp.where(lane == 1, skip, 0.0)))
            gated = jnp.where(lane == 0, lanes_of(c, 1), jnp.where(lane == 1, lanes_of(c, 2), aux_ref[at])) * mixed
            old = rows_ref[at, 128:].astype(F32)
            after = jnp.where(lane == 0, old + lanes_of(c, 3) * taps[g:g + 1, 127:128], old)
            square = gated * gated
            total0 = total0 + square[:8] + square[8:]
            square = after * after
            total1 = total1 + square[:8] + square[8:]
            out_ref[at, :128] = gated.astype(BF)
            out_ref[at, 128:] = after.astype(BF)
    acc[0], acc[1] = total0, total1

    @pl.when(step == pl.num_programs(0) - 1)
    def _():
        row0 = jnp.sum(acc[0], axis=0, keepdims=True)
        row1 = jnp.sum(acc[1], axis=0, keepdims=True)
        one = lax.broadcasted_iota(jnp.int32, (1, 128), 1)
        sq_ref[...] = jnp.concatenate(
            [row0, jnp.where(one == 0, row1, later_ref[:, :128]), later_ref[:, 128:]], axis=1)


def sf_spec(c):
    return pl.BlockSpec((3, 3, c), lambda i: (0, 0, i))


def tail(docs, base, gate, key, value, sf):
    ch, n = gate.shape
    c = min(BL, ch)
    wide = pl.BlockSpec((c, 256), lambda i: (i, n // 256 - 1))
    return pl.pallas_call(
        tail_kernel, grid=(ch // c,),
        in_specs=[SMEM, SMEM, wide, wide, wide, sf_spec(c)],
        out_specs=pl.BlockSpec((c // CB, ENDS, 128), lambda i: (i, 0, 0)),
        out_shape=jax.ShapeDtypeStruct((ch // CB, ENDS, 128), BF),
        scratch_shapes=[pltpu.VMEM((2, GROUP, 128), BF)],
        compiler_params=pltpu.CompilerParams(vmem_limit_bytes=LATER_VMEM), name="tail",
    )(docs, base, gate, key, value, sf)


def param_specs(c):
    row = pl.BlockSpec((1, c), lambda i: (0, i))
    return [sf_spec(c), row, pl.BlockSpec((c // GROUP, MR), lambda i: (i, 0))]


def later(docs, base, gate, key, value, sf, skip, taps):
    ch, n = gate.shape
    c = min(BL, ch)
    wide = pl.BlockSpec((c, n), lambda i: (i, 0))
    tile = pl.BlockSpec((c, 128), lambda i: (i, 0))
    return pl.pallas_call(
        later_kernel, grid=(ch // c,),
        in_specs=[SMEM, SMEM, wide, wide, wide] + param_specs(c),
        out_specs=[wide, tile, tile, pl.BlockSpec((c // CB, 16, CB), lambda i: (i, 0, 0)),
                   pl.BlockSpec((c // GROUP, MR, MR), lambda i: (i, 0, 0)), pl.BlockSpec((1, n - 128), lambda i: (0, 0))],
        out_shape=[pltpu.HBM((ch, n), BF), jax.ShapeDtypeStruct((ch, 128), F32),
                   jax.ShapeDtypeStruct((ch, 128), BF), jax.ShapeDtypeStruct((ch // CB, 16, CB), BF),
                   jax.ShapeDtypeStruct((ch // GROUP, MR, MR), BF), jax.ShapeDtypeStruct((1, n - 128), F32)],
        scratch_shapes=[pltpu.VMEM((3, 256, 128), BF), pltpu.VMEM((2, GROUP, n), BF), pltpu.VMEM((GROUP, 128), BF),
                        pltpu.VMEM((8, n - 128), F32)],
        cost_estimate=pl.CostEstimate(flops=2 * ch * 384 * 256 * 8, bytes_accessed=8 * ch * n, transcendentals=0),
        compiler_params=pltpu.CompilerParams(vmem_limit_bytes=LATER_VMEM), name="later",
    )(docs, base, gate, key, value, sf, skip, taps)


def first(docs, base, halo, done, sf, skip, taps):
    done = [pltpu.with_memory_space_constraint(x, pltpu.HBM if i == 0 else pltpu.VMEM) for i, x in enumerate(done)]
    rows, aux, prod, own, rings, squares = done
    ch, n = rows.shape
    c = min(BL, ch)
    half = pl.BlockSpec((c, 256), lambda i: (i, 0))
    tile = pl.BlockSpec((c, 128), lambda i: (i, 0))
    whole = lambda w: pl.BlockSpec((1, w), lambda i: (0, 0))
    return pl.pallas_call(
        first_kernel, grid=(ch // c,),
        in_specs=[SMEM, SMEM, pl.BlockSpec((c // CB, ENDS, 128), lambda i: (i, 0, 0)), half, tile, tile,
                  pl.BlockSpec((c // CB, 16, CB), lambda i: (i, 0, 0)),
                  pl.BlockSpec((c // GROUP, MR, MR), lambda i: (i, 0, 0)), whole(n - 128)] + param_specs(c),
        out_specs=[half, whole(n)],
        out_shape=[jax.ShapeDtypeStruct((ch, n), BF), jax.ShapeDtypeStruct((1, n), F32)],
        scratch_shapes=[pltpu.VMEM((256, 128), BF), pltpu.VMEM((8, 128), F32), pltpu.VMEM((2, 8, 128), F32)],
        input_output_aliases={3: 0},
        cost_estimate=pl.CostEstimate(flops=2 * ch * 128 * 256 * 8, bytes_accessed=4 * ch * n, transcendentals=0),
        compiler_params=pltpu.CompilerParams(vmem_limit_bytes=FIRST_VMEM), name="first",
    )(docs, base, halo, rows, aux, prod, own, rings, squares, sf, skip, taps)


FIRST_VMEM = 24 << 20
LATER_VMEM = 40 << 20
def final_kernel(recv_ref, sums_ref, gain_ref, out_ref):
    per, c, n = recv_ref.shape
    gain = jnp.broadcast_to(gain_ref[...], (c, n))
    for i in range(per):
        scale = lax.rsqrt(sums_ref[i] / D + EPS)
        out_ref[:, n * i:n * (i + 1)] = (recv_ref[i].astype(F32) * scale * gain).astype(BF)


def final(recv, sums, gain):
    k, c, n = recv.shape
    per = min(k, PER)
    return pl.pallas_call(
        final_kernel, grid=(k // per,),
        in_specs=[pl.BlockSpec((per, c, n), lambda i: (i, 0, 0)), pl.BlockSpec((per, 1, n), lambda i: (i, 0, 0)),
                  pl.BlockSpec((c, 1), lambda i: (0, 0))],
        out_specs=pl.BlockSpec((c, per * n), lambda i: (0, i)),
        out_shape=jax.ShapeDtypeStruct((c, k * n), BF),
        compiler_params=pltpu.CompilerParams(vmem_limit_bytes=24 << 20), name="settle",
    )(recv, sums, gain)


ROUNDS = (((0, 1), (2, 3), (4, 5), (6, 7)), ((1, 2), (3, 4), (5, 6), (7, 0)), ((0, 3), (7, 4), (1, 6), (2, 5)))


def channel_sum(x):
    if lax.axis_size("ch") != 8:
        return lax.psum(x, "ch"), jnp.zeros_like(x)
    for pairs in ROUNDS[:-1]:
        x = x + lax.ppermute(x, "ch", list(pairs) + [(b, a) for a, b in pairs])
    return x, lax.ppermute(x, "ch", list(ROUNDS[-1]) + [(b, a) for a, b in ROUNDS[-1]])


def local(gate, key, value, sf, taps, skip, gain, docs):
    place = lax.axis_index("ctx")
    width = lax.axis_size("ctx")
    ch, n = gate.shape
    base = (place * n).astype(jnp.int32).reshape(1)
    skip = skip.reshape(1, ch)
    gain = lax.dynamic_slice_in_dim(gain, place * (ch // width), ch // width).reshape(ch // width, 1)
    gate, key, value = (pltpu.with_memory_space_constraint(x, pltpu.HBM) for x in (gate, key, value))
    ends = tail(pltpu.with_memory_space_constraint(docs, pltpu.HBM), base, gate, key, value, pltpu.with_memory_space_constraint(sf, pltpu.HBM))
    halo = lax.ppermute(ends, "ctx", [(i, i + 1) for i in range(width - 1)])
    done = later(docs, base, gate, key, value, sf, skip, taps)
    rows, squares = first(docs, base, halo, done, sf, skip, taps)
    recv = lax.all_to_all(rows.reshape(width, ch // width, n), "ctx", split_axis=0, concat_axis=0, tiled=True)
    near, far = channel_sum(squares)
    far, recv = lax.optimization_barrier((far, recv))
    sums = lax.all_to_all(jnp.broadcast_to((near + far)[None], (width, 1, n)), "ctx", split_axis=0, concat_axis=0, tiled=True)
    return final(recv, sums, gain)


def solution(mesh):
    in_specs = (P("ch", "ctx"),) * 3 + (P(None, None, "ch"), P("ch", None), P("ch"), P("ch"), P())
    return jax.shard_map(local, mesh=mesh, in_specs=in_specs, out_specs=P(("ch", "ctx"), None), check_vma=False)
```

```python
import jax
import jax.numpy as jnp
from jax import lax
from jax.experimental import pallas as pl
from jax.experimental.pallas import tpu as pltpu
from jax.sharding import PartitionSpec as P

D = 8192
GROUP = 16
MR = 128
EPS = 1e-6
DOCS = 64
F32 = jnp.float32
BF = jnp.bfloat16
CB = 128
BL = 512
ENDS = 144
PER = 16
BIG = 56 << 20
SMEM = pl.BlockSpec(memory_space=pltpu.SMEM)


def starts_row(docs_ref, base, count):
    pos = lax.broadcasted_iota(jnp.int32, (1, count), 1) + base
    first = jnp.int32(0)
    start = jnp.zeros((1, count), jnp.int32)
    for d in range(DOCS):
        start = jnp.where(pos >= first, first, start)
        first = first + docs_ref[d]
    return pos, start


def as_bf(flag, shape):
    return jnp.broadcast_to(flag.astype(F32), shape).astype(BF)


def tile_masks(first):
    s = lax.broadcasted_iota(jnp.int32, (128, 128), 0)
    t = lax.broadcasted_iota(jnp.int32, (128, 128), 1)
    return (((s > t) & (s - 128 >= first)).astype(F32).astype(BF), ((s <= t) & (s >= first)).astype(F32).astype(BF))


def spread(rows):
    count = sum(r.shape[0] for r in rows)
    rest = jnp.concatenate(rows + [jnp.zeros((16 - count, CB), F32)], axis=0)
    pieces = []
    for _ in range(3):
        pieces.append(rest.astype(BF))
        rest = rest - pieces[-1].astype(F32)
    row = lax.broadcasted_iota(jnp.int32, (16, 128 * count), 0)
    column = lax.broadcasted_iota(jnp.int32, (16, 128 * count), 1)
    ones = ((column >= 128 * row) & (column < 128 * row + 128)).astype(F32).astype(BF)
    return lax.dot_general(jnp.concatenate(pieces, axis=0), jnp.concatenate([ones] * 3, axis=0),
                           (((0,), (0,)), ((), ())), preferred_element_type=F32)


def lanes_of(wide, i, tiles=1):
    part = wide[:, 128 * i:128 * (i + 1)]
    return part if tiles == 1 else jnp.concatenate([part] * tiles, axis=1)


def conv3(raw, keeps, cols, first):
    one = pltpu.roll(raw, 1, 1) * keeps[0]
    two = pltpu.roll(raw, 2, 1) * keeps[1]
    k = raw.shape[1] // 128
    return (lanes_of(cols, first, k) * raw.astype(F32) + lanes_of(cols, first + 1, k) * one.astype(F32)
            + lanes_of(cols, first + 2, k) * two.astype(F32))


def ring_of(taps):
    return pltpu.roll(jnp.broadcast_to(taps, (128, 128)), 0, 1, stride=1, stride_axis=0).astype(BF)


def pick(here, *wanted):
    row = lax.broadcasted_iota(jnp.int32, (16, 128), 0)
    lane = lax.broadcasted_iota(jnp.int32, (16, 128), 1)
    out = jnp.zeros((16, CB), F32)
    for ref, lanes, at, first, count in wanted:
        one_hot = ((lane - first == row - at) & (row >= at) & (row < at + count)).astype(F32).astype(BF)
        out = out + lax.dot_general(one_hot, ref[here, lanes], (((1,), (1,)), ((), ())), preferred_element_type=F32)
    return out.astype(BF)


def tail_kernel(docs_ref, base_ref, gate_ref, key_ref, value_ref, sf_ref, out_ref, keeps):
    @pl.when(pl.program_id(0) == 0)
    def _():
        pos, start = starts_row(docs_ref, base_ref[0] + 384, 128)
        for lag in (1, 2):
            keeps[lag - 1] = as_bf(pos - lag >= start, (GROUP, 128))

    last = lax.broadcasted_iota(jnp.int32, (GROUP, 128), 1) == 127

    def filtered(ref, at, cols, i):
        raw = ref[at, 128:]
        one = pltpu.roll(raw, 1, 1) * keeps[0]
        two = pltpu.roll(jnp.where(last, ref[at, :128], raw), 2, 1) * keeps[1]
        return (lanes_of(cols, i) * raw.astype(F32) + lanes_of(cols, i + 1) * one.astype(F32)
                + lanes_of(cols, i + 2) * two.astype(F32))

    for b in range(gate_ref.shape[0] // CB):
        here = slice(CB * b, CB * (b + 1))
        sf = sf_ref[:, :, here]
        cols = spread([sf[1], sf[2]])
        for g in range(CB // GROUP):
            at = slice(CB * b + GROUP * g, CB * b + GROUP * (g + 1))
            c = cols[GROUP * g:GROUP * (g + 1)]
            out_ref[b, GROUP * g:GROUP * (g + 1)] = (filtered(key_ref, at, c, 0) * filtered(value_ref, at, c, 3)).astype(BF)
        lanes = slice(128, 256)
        out_ref[b, CB:] = pick(here, (gate_ref, lanes, 0, 126, 2), (key_ref, lanes, 2, 126, 2), (value_ref, lanes, 4, 126, 2))


def later_kernel(docs_ref, base_ref, gate_ref, key_ref, value_ref, sf_ref, skip_ref, taps_ref,
                 out_ref, aux_ref, prod_ref, own_ref, ring_ref, sq_ref, masks, keeps, inner, acc):
    step = pl.program_id(0)

    @pl.when(step == 0)
    def _():
        pos, start = starts_row(docs_ref, base_ref[0], 512)
        rel = pos - base_ref[0]
        for lag in (1, 2):
            keeps[lag - 1] = as_bf((pos - lag >= start) & (rel >= lag), (GROUP, 512))
        inner[...] = as_bf(rel[:, :128] >= 2, (GROUP, 128))
        for j in range(3):
            first = start[:, 128 * (j + 1):128 * (j + 2)] - (base_ref[0] + 128 * (j + 1))
            masks[j, :128, :], masks[j, 128:, :] = tile_masks(jnp.broadcast_to(first, (128, 128)))
        acc[...] = jnp.zeros_like(acc)

    total = acc[...]
    for b in range(gate_ref.shape[0] // CB):
        here = slice(CB * b, CB * (b + 1))
        sf = sf_ref[:, :, here]
        cols = spread([sf[0], sf[1], sf[2], skip_ref[:, here]])
        taps = taps_ref[8 * b:8 * (b + 1)].astype(BF).astype(F32)
        for g in range(CB // GROUP):
            at = slice(CB * b + GROUP * g, CB * b + GROUP * (g + 1))
            c = cols[GROUP * g:GROUP * (g + 1)]
            product = (conv3(key_ref[at], keeps, c, 3) * conv3(value_ref[at], keeps, c, 6)).astype(BF)
            product = jnp.concatenate([product[:, :128] * inner[...], product[:, 128:]], axis=1)
            prod_ref[at] = product[:, :128]
            gate = conv3(gate_ref[at], keeps, c, 0)
            ring = ring_of(taps[g:g + 1])
            ring_ref[8 * b + g] = ring
            both = jnp.concatenate([ring, ring], axis=0)
            mixed = jnp.concatenate([
                jnp.dot(product[:, 128 * j:128 * j + 256], both * masks[j], preferred_element_type=F32)
                for j in range(3)], axis=1)
            mixed = mixed + lanes_of(c, 9, 3) * product[:, 128:].astype(F32)
            gated = gate[:, 128:] * mixed
            aux_ref[at] = gate[:, :128]
            square = gated * gated
            total = total + square[:8] + square[8:]
            out_ref[at, 128:] = gated.astype(BF)
            out_ref[at, :128] = jnp.zeros((GROUP, 128), BF)
        tile0, tile1 = slice(0, 128), slice(128, 256)
        own_ref[b] = pick(here, (gate_ref, tile0, 0, 0, 2), (key_ref, tile0, 2, 0, 2), (value_ref, tile0, 4, 0, 2),
                          (gate_ref, tile0, 6, 126, 2), (gate_ref, tile1, 8, 0, 1))
    acc[...] = total

    @pl.when(step == pl.num_programs(0) - 1)
    def _():
        sq_ref[...] = jnp.sum(acc[...], axis=0, keepdims=True)


def first_kernel(docs_ref, base_ref, halo_ref, rows_ref, aux_ref, prod_ref, own_ref, ring_ref, later_ref, sf_ref, skip_ref,
                 taps_ref, out_ref, sq_ref, masks, keeps, acc):
    step = pl.program_id(0)

    @pl.when(step == 0)
    def _():
        pos, start = starts_row(docs_ref, base_ref[0], 256)
        for lag in (1, 2):
            keeps[lag - 1:lag] = (pos[:, :128] - lag >= start[:, :128]).astype(F32)
        for lag in (1, 2, 127):
            row = 1 + lag if lag < 3 else 4
            keeps[row:row + 1] = (pos[:, 128:] - lag >= start[:, 128:]).astype(F32)
        masks[:128], masks[128:] = tile_masks(jnp.broadcast_to(start[:, :128] - base_ref[0], (128, 128)))
        acc[...] = jnp.zeros_like(acc)

    lane = lax.broadcasted_iota(jnp.int32, (GROUP, 128), 1)
    total0, total1 = acc[0], acc[1]
    for b in range(halo_ref.shape[0]):
        here = slice(CB * b, CB * (b + 1))
        own = own_ref[b].astype(F32)
        past = halo_ref[b, CB:].astype(F32)

        def both_positions(i):
            t = [sf_ref[i, lag:lag + 1, here] for lag in range(3)]
            x = own[2 * i:2 * i + 2]
            h = past[2 * i:2 * i + 2]
            at0 = t[0] * x[:1] + keeps[0:1, 0:1] * (t[1] * h[1:]) + keeps[1:2, 0:1] * (t[2] * h[:1])
            at1 = t[0] * x[1:] + keeps[0:1, 1:2] * (t[1] * x[:1]) + keeps[1:2, 1:2] * (t[2] * h[1:])
            return jnp.concatenate([at0, at1], axis=0)

        two = (both_positions(1) * both_positions(2)).astype(BF).astype(F32)
        t = [sf_ref[0, lag:lag + 1, here] for lag in range(3)]
        gate = t[0] * own[8:9] + keeps[2:3, 0:1] * (t[1] * own[7:8]) + keeps[3:4, 0:1] * (t[2] * own[6:7])
        cols = spread([skip_ref[:, here], both_positions(0), keeps[4:5, 0:1] * two[1:] * gate, two])
        taps = taps_ref[8 * b:8 * (b + 1)].astype(BF).astype(F32)
        for g in range(CB // GROUP):
            at = slice(CB * b + GROUP * g, CB * b + GROUP * (g + 1))
            inside = slice(GROUP * g, GROUP * (g + 1))
            c = cols[inside]
            product = prod_ref[at]
            ring = ring_ref[8 * b + g]
            mixed = jnp.dot(jnp.concatenate([halo_ref[b, inside], product], axis=1),
                            jnp.concatenate([ring, ring], axis=0) * masks[...], preferred_element_type=F32)
            skip = lanes_of(c, 0)
            near = ring[:16].astype(F32) * masks[128:144].astype(F32)
            mixed = (mixed + skip * product.astype(F32)
                     + lanes_of(c, 4) * (near[0:1] + jnp.where(lane == 0, skip, 0.0))
                     + lanes_of(c, 5) * (near[1:2] + jnp.where(lane == 1, skip, 0.0)))
            gated = jnp.where(lane == 0, lanes_of(c, 1), jnp.where(lane == 1, lanes_of(c, 2), aux_ref[at])) * mixed
            old = rows_ref[at, 128:].astype(F32)
            after = jnp.where(lane == 0, old + lanes_of(c, 3) * taps[g:g + 1, 127:128], old)
            square = gated * gated
            total0 = total0 + square[:8] + square[8:]
            square = after * after
            total1 = total1 + square[:8] + square[8:]
            out_ref[at, :128] = gated.astype(BF)
            out_ref[at, 128:] = after.astype(BF)
    acc[0], acc[1] = total0, total1

    @pl.when(step == pl.num_programs(0) - 1)
    def _():
        row0 = jnp.sum(acc[0], axis=0, keepdims=True)
        row1 = jnp.sum(acc[1], axis=0, keepdims=True)
        one = lax.broadcasted_iota(jnp.int32, (1, 128), 1)
        sq_ref[...] = jnp.concatenate(
            [row0, jnp.where(one == 0, row1, later_ref[:, :128]), later_ref[:, 128:]], axis=1)


def sf_spec(c):
    return pl.BlockSpec((3, 3, c), lambda i: (0, 0, i))


def tail(docs, base, gate, key, value, sf):
    ch, n = gate.shape
    c = min(BL, ch)
    wide = pl.BlockSpec((c, 256), lambda i: (i, n // 256 - 1))
    return pl.pallas_call(
        tail_kernel, grid=(ch // c,),
        in_specs=[SMEM, SMEM, wide, wide, wide, sf_spec(c)],
        out_specs=pl.BlockSpec((c // CB, ENDS, 128), lambda i: (i, 0, 0)),
        out_shape=jax.ShapeDtypeStruct((ch // CB, ENDS, 128), BF),
        scratch_shapes=[pltpu.VMEM((2, GROUP, 128), BF)],
        compiler_params=pltpu.CompilerParams(vmem_limit_bytes=LATER_VMEM), name="tail",
    )(docs, base, gate, key, value, sf)


def param_specs(c):
    row = pl.BlockSpec((1, c), lambda i: (0, i))
    return [sf_spec(c), row, pl.BlockSpec((c // GROUP, MR), lambda i: (i, 0))]


def later(docs, base, gate, key, value, sf, skip, taps):
    ch, n = gate.shape
    c = min(BL, ch)
    wide = pl.BlockSpec((c, n), lambda i: (i, 0))
    tile = pl.BlockSpec((c, 128), lambda i: (i, 0))
    return pl.pallas_call(
        later_kernel, grid=(ch // c,),
        in_specs=[SMEM, SMEM, wide, wide, wide] + param_specs(c),
        out_specs=[wide, tile, tile, pl.BlockSpec((c // CB, 16, CB), lambda i: (i, 0, 0)),
                   pl.BlockSpec((c // GROUP, MR, MR), lambda i: (i, 0, 0)), pl.BlockSpec((1, n - 128), lambda i: (0, 0))],
        out_shape=[pltpu.HBM((ch, n), BF), jax.ShapeDtypeStruct((ch, 128), F32),
                   jax.ShapeDtypeStruct((ch, 128), BF), jax.ShapeDtypeStruct((ch // CB, 16, CB), BF),
                   jax.ShapeDtypeStruct((ch // GROUP, MR, MR), BF), jax.ShapeDtypeStruct((1, n - 128), F32)],
        scratch_shapes=[pltpu.VMEM((3, 256, 128), BF), pltpu.VMEM((2, GROUP, n), BF), pltpu.VMEM((GROUP, 128), BF),
                        pltpu.VMEM((8, n - 128), F32)],
        cost_estimate=pl.CostEstimate(flops=2 * ch * 384 * 256 * 8, bytes_accessed=8 * ch * n, transcendentals=0),
        compiler_params=pltpu.CompilerParams(vmem_limit_bytes=LATER_VMEM), name="later",
    )(docs, base, gate, key, value, sf, skip, taps)


def first(docs, base, halo, done, sf, skip, taps):
    done = [pltpu.with_memory_space_constraint(x, pltpu.HBM if i == 0 else pltpu.VMEM) for i, x in enumerate(done)]
    rows, aux, prod, own, rings, squares = done
    ch, n = rows.shape
    c = min(BL, ch)
    half = pl.BlockSpec((c, 256), lambda i: (i, 0))
    tile = pl.BlockSpec((c, 128), lambda i: (i, 0))
    whole = lambda w: pl.BlockSpec((1, w), lambda i: (0, 0))
    return pl.pallas_call(
        first_kernel, grid=(ch // c,),
        in_specs=[SMEM, SMEM, pl.BlockSpec((c // CB, ENDS, 128), lambda i: (i, 0, 0)), half, tile, tile,
                  pl.BlockSpec((c // CB, 16, CB), lambda i: (i, 0, 0)),
                  pl.BlockSpec((c // GROUP, MR, MR), lambda i: (i, 0, 0)), whole(n - 128)] + param_specs(c),
        out_specs=[half, whole(n)],
        out_shape=[jax.ShapeDtypeStruct((ch, n), BF), jax.ShapeDtypeStruct((1, n), F32)],
        scratch_shapes=[pltpu.VMEM((256, 128), BF), pltpu.VMEM((8, 128), F32), pltpu.VMEM((2, 8, 128), F32)],
        input_output_aliases={3: 0},
        cost_estimate=pl.CostEstimate(flops=2 * ch * 128 * 256 * 8, bytes_accessed=4 * ch * n, transcendentals=0),
        compiler_params=pltpu.CompilerParams(vmem_limit_bytes=FIRST_VMEM), name="first",
    )(docs, base, halo, rows, aux, prod, own, rings, squares, sf, skip, taps)


FIRST_VMEM = 24 << 20
LATER_VMEM = 40 << 20
def final_kernel(recv_ref, sums_ref, gain_ref, out_ref):
    per, c, n = recv_ref.shape
    gain = jnp.broadcast_to(gain_ref[...], (c, n))
    for i in range(per):
        scale = lax.rsqrt(sums_ref[i] / D + EPS)
        out_ref[:, n * i:n * (i + 1)] = (recv_ref[i].astype(F32) * scale * gain).astype(BF)


def final(recv, sums, gain):
    k, c, n = recv.shape
    per = min(k, PER)
    return pl.pallas_call(
        final_kernel, grid=(k // per,),
        in_specs=[pl.BlockSpec((per, c, n), lambda i: (i, 0, 0)), pl.BlockSpec((per, 1, n), lambda i: (i, 0, 0)),
                  pl.BlockSpec((c, 1), lambda i: (0, 0))],
        out_specs=pl.BlockSpec((c, per * n), lambda i: (0, i)),
        out_shape=jax.ShapeDtypeStruct((c, k * n), BF),
        compiler_params=pltpu.CompilerParams(vmem_limit_bytes=24 << 20), name="settle",
    )(recv, sums, gain)


ROUNDS = (((0, 1), (2, 3), (4, 5), (6, 7)), ((1, 2), (3, 4), (5, 6), (7, 0)), ((0, 3), (7, 4), (1, 6), (2, 5)))


def channel_sum(x):
    if lax.axis_size("ch") != 8:
        return lax.psum(x, "ch"), jnp.zeros_like(x)
    for pairs in ROUNDS[:-1]:
        x = x + lax.ppermute(x, "ch", list(pairs) + [(b, a) for a, b in pairs])
    return x, lax.ppermute(x, "ch", list(ROUNDS[-1]) + [(b, a) for a, b in ROUNDS[-1]])


def copies_kernel(near_ref, far_ref, out_ref):
    total = near_ref[...] + far_ref[...]
    for i in range(out_ref.shape[0]):
        out_ref[i] = total


def copies(near, far, count):
    return pl.pallas_call(
        copies_kernel, out_shape=jax.ShapeDtypeStruct((count,) + near.shape, F32),
        compiler_params=pltpu.CompilerParams(vmem_limit_bytes=8 << 20), name="copies",
    )(near, far)


def local(gate, key, value, sf, taps, skip, gain, docs):
    place = lax.axis_index("ctx")
    width = lax.axis_size("ctx")
    ch, n = gate.shape
    base = (place * n).astype(jnp.int32).reshape(1)
    skip = skip.reshape(1, ch)
    gain = lax.dynamic_slice_in_dim(gain, place * (ch // width), ch // width).reshape(ch // width, 1)
    gate, key, value = (pltpu.with_memory_space_constraint(x, pltpu.HBM) for x in (gate, key, value))
    ends = tail(pltpu.with_memory_space_constraint(docs, pltpu.HBM), base, gate, key, value, pltpu.with_memory_space_constraint(sf, pltpu.HBM))
    halo = lax.ppermute(ends, "ctx", [(i, i + 1) for i in range(width - 1)])
    done = later(docs, base, gate, key, value, sf, skip, taps)
    rows, squares = first(docs, base, halo, done, sf, skip, taps)
    recv = lax.all_to_all(rows.reshape(width, ch // width, n), "ctx", split_axis=0, concat_axis=0, tiled=True)
    near, far = channel_sum(squares)
    total = copies(near, far, width)
    total, recv = lax.optimization_barrier((total, recv))
    sums = lax.all_to_all(total, "ctx", split_axis=0, concat_axis=0, tiled=True)
    return final(recv, sums, gain)


def solution(mesh):
    in_specs = (P("ch", "ctx"),) * 3 + (P(None, None, "ch"), P("ch", None), P("ch"), P("ch"), P())
    return jax.shard_map(local, mesh=mesh, in_specs=in_specs, out_specs=P(("ch", "ctx"), None), check_vma=False)
```

```python
import jax
import jax.numpy as jnp
from jax import lax
from jax.experimental import pallas as pl
from jax.experimental.pallas import tpu as pltpu
from jax.sharding import PartitionSpec as P

D = 8192
GROUP = 16
MR = 128
EPS = 1e-6
DOCS = 64
F32 = jnp.float32
BF = jnp.bfloat16
CB = 128
BL = 512
ENDS = 144
PER = 16
BIG = 56 << 20
SMEM = pl.BlockSpec(memory_space=pltpu.SMEM)


def starts_row(docs_ref, base, count):
    pos = lax.broadcasted_iota(jnp.int32, (1, count), 1) + base
    first = jnp.int32(0)
    start = jnp.zeros((1, count), jnp.int32)
    for d in range(DOCS):
        start = jnp.where(pos >= first, first, start)
        first = first + docs_ref[d]
    return pos, start


def as_bf(flag, shape):
    return jnp.broadcast_to(flag.astype(F32), shape).astype(BF)


def tile_masks(first):
    s = lax.broadcasted_iota(jnp.int32, (128, 128), 0)
    t = lax.broadcasted_iota(jnp.int32, (128, 128), 1)
    return (((s > t) & (s - 128 >= first)).astype(F32).astype(BF), ((s <= t) & (s >= first)).astype(F32).astype(BF))


def spread(rows):
    count = sum(r.shape[0] for r in rows)
    rest = jnp.concatenate(rows + [jnp.zeros((16 - count, CB), F32)], axis=0)
    pieces = []
    for _ in range(3):
        pieces.append(rest.astype(BF))
        rest = rest - pieces[-1].astype(F32)
    row = lax.broadcasted_iota(jnp.int32, (16, 128 * count), 0)
    column = lax.broadcasted_iota(jnp.int32, (16, 128 * count), 1)
    ones = ((column >= 128 * row) & (column < 128 * row + 128)).astype(F32).astype(BF)
    return lax.dot_general(jnp.concatenate(pieces, axis=0), jnp.concatenate([ones] * 3, axis=0),
                           (((0,), (0,)), ((), ())), preferred_element_type=F32)


def lanes_of(wide, i, tiles=1):
    part = wide[:, 128 * i:128 * (i + 1)]
    return part if tiles == 1 else jnp.concatenate([part] * tiles, axis=1)


def conv3(raw, keeps, cols, first):
    one = pltpu.roll(raw, 1, 1) * keeps[0]
    two = pltpu.roll(raw, 2, 1) * keeps[1]
    k = raw.shape[1] // 128
    return (lanes_of(cols, first, k) * raw.astype(F32) + lanes_of(cols, first + 1, k) * one.astype(F32)
            + lanes_of(cols, first + 2, k) * two.astype(F32))


def ring_of(taps):
    return pltpu.roll(jnp.broadcast_to(taps, (128, 128)), 0, 1, stride=1, stride_axis=0).astype(BF)


def pick(here, *wanted):
    row = lax.broadcasted_iota(jnp.int32, (16, 128), 0)
    lane = lax.broadcasted_iota(jnp.int32, (16, 128), 1)
    out = jnp.zeros((16, CB), F32)
    for ref, lanes, at, first, count in wanted:
        one_hot = ((lane - first == row - at) & (row >= at) & (row < at + count)).astype(F32).astype(BF)
        out = out + lax.dot_general(one_hot, ref[here, lanes], (((1,), (1,)), ((), ())), preferred_element_type=F32)
    return out.astype(BF)


def tail_kernel(docs_ref, base_ref, gate_ref, key_ref, value_ref, sf_ref, out_ref, keeps):
    @pl.when(pl.program_id(0) == 0)
    def _():
        pos, start = starts_row(docs_ref, base_ref[0] + 384, 128)
        for lag in (1, 2):
            keeps[lag - 1] = as_bf(pos - lag >= start, (GROUP, 128))

    last = lax.broadcasted_iota(jnp.int32, (GROUP, 128), 1) == 127

    def filtered(ref, at, cols, i):
        raw = ref[at, 128:]
        one = pltpu.roll(raw, 1, 1) * keeps[0]
        two = pltpu.roll(jnp.where(last, ref[at, :128], raw), 2, 1) * keeps[1]
        return (lanes_of(cols, i) * raw.astype(F32) + lanes_of(cols, i + 1) * one.astype(F32)
                + lanes_of(cols, i + 2) * two.astype(F32))

    for b in range(gate_ref.shape[0] // CB):
        here = slice(CB * b, CB * (b + 1))
        sf = sf_ref[:, :, here]
        cols = spread([sf[1], sf[2]])
        for g in range(CB // GROUP):
            at = slice(CB * b + GROUP * g, CB * b + GROUP * (g + 1))
            c = cols[GROUP * g:GROUP * (g + 1)]
            out_ref[b, GROUP * g:GROUP * (g + 1)] = (filtered(key_ref, at, c, 0) * filtered(value_ref, at, c, 3)).astype(BF)
        lanes = slice(128, 256)
        out_ref[b, CB:] = pick(here, (gate_ref, lanes, 0, 126, 2), (key_ref, lanes, 2, 126, 2), (value_ref, lanes, 4, 126, 2))


def later_kernel(docs_ref, base_ref, gate_ref, key_ref, value_ref, sf_ref, skip_ref, taps_ref,
                 out_ref, aux_ref, prod_ref, own_ref, ring_ref, sq_ref, masks, keeps, inner, acc):
    step = pl.program_id(0)

    @pl.when(step == 0)
    def _():
        pos, start = starts_row(docs_ref, base_ref[0], 512)
        rel = pos - base_ref[0]
        for lag in (1, 2):
            keeps[lag - 1] = as_bf((pos - lag >= start) & (rel >= lag), (GROUP, 512))
        inner[...] = as_bf(rel[:, :128] >= 2, (GROUP, 128))
        for j in range(3):
            first = start[:, 128 * (j + 1):128 * (j + 2)] - (base_ref[0] + 128 * (j + 1))
            masks[j, :128, :], masks[j, 128:, :] = tile_masks(jnp.broadcast_to(first, (128, 128)))
        acc[...] = jnp.zeros_like(acc)

    total = acc[...]
    for b in range(gate_ref.shape[0] // CB):
        here = slice(CB * b, CB * (b + 1))
        sf = sf_ref[:, :, here]
        cols = spread([sf[0], sf[1], sf[2], skip_ref[:, here]])
        taps = taps_ref[8 * b:8 * (b + 1)].astype(BF).astype(F32)
        for g in range(CB // GROUP):
            at = slice(CB * b + GROUP * g, CB * b + GROUP * (g + 1))
            c = cols[GROUP * g:GROUP * (g + 1)]
            product = (conv3(key_ref[at], keeps, c, 3) * conv3(value_ref[at], keeps, c, 6)).astype(BF)
            product = jnp.concatenate([product[:, :128] * inner[...], product[:, 128:]], axis=1)
            prod_ref[at] = product[:, :128]
            gate = conv3(gate_ref[at], keeps, c, 0)
            ring = ring_of(taps[g:g + 1])
            ring_ref[8 * b + g] = ring
            both = jnp.concatenate([ring, ring], axis=0)
            mixed = jnp.concatenate([
                jnp.dot(product[:, 128 * j:128 * j + 256], both * masks[j], preferred_element_type=F32)
                for j in range(3)], axis=1)
            mixed = mixed + lanes_of(c, 9, 3) * product[:, 128:].astype(F32)
            gated = gate[:, 128:] * mixed
            aux_ref[at] = gate[:, :128]
            square = gated * gated
            total = total + square[:8] + square[8:]
            out_ref[at, 128:] = gated.astype(BF)
            out_ref[at, :128] = jnp.zeros((GROUP, 128), BF)
        tile0, tile1 = slice(0, 128), slice(128, 256)
        own_ref[b] = pick(here, (gate_ref, tile0, 0, 0, 2), (key_ref, tile0, 2, 0, 2), (value_ref, tile0, 4, 0, 2),
                          (gate_ref, tile0, 6, 126, 2), (gate_ref, tile1, 8, 0, 1))
    acc[...] = total

    @pl.when(step == pl.num_programs(0) - 1)
    def _():
        sq_ref[...] = jnp.sum(acc[...], axis=0, keepdims=True)


def first_kernel(docs_ref, base_ref, halo_ref, rows_ref, aux_ref, prod_ref, own_ref, ring_ref, later_ref, sf_ref, skip_ref,
                 taps_ref, out_ref, sq_ref, masks, keeps, acc):
    step = pl.program_id(0)

    @pl.when(step == 0)
    def _():
        pos, start = starts_row(docs_ref, base_ref[0], 256)
        for lag in (1, 2):
            keeps[lag - 1:lag] = (pos[:, :128] - lag >= start[:, :128]).astype(F32)
        for lag in (1, 2, 127):
            row = 1 + lag if lag < 3 else 4
            keeps[row:row + 1] = (pos[:, 128:] - lag >= start[:, 128:]).astype(F32)
        masks[:128], masks[128:] = tile_masks(jnp.broadcast_to(start[:, :128] - base_ref[0], (128, 128)))
        acc[...] = jnp.zeros_like(acc)

    lane = lax.broadcasted_iota(jnp.int32, (GROUP, 128), 1)
    total0, total1 = acc[0], acc[1]
    for b in range(halo_ref.shape[0]):
        here = slice(CB * b, CB * (b + 1))
        own = own_ref[b].astype(F32)
        past = halo_ref[b, CB:].astype(F32)

        def both_positions(i):
            t = [sf_ref[i, lag:lag + 1, here] for lag in range(3)]
            x = own[2 * i:2 * i + 2]
            h = past[2 * i:2 * i + 2]
            at0 = t[0] * x[:1] + keeps[0:1, 0:1] * (t[1] * h[1:]) + keeps[1:2, 0:1] * (t[2] * h[:1])
            at1 = t[0] * x[1:] + keeps[0:1, 1:2] * (t[1] * x[:1]) + keeps[1:2, 1:2] * (t[2] * h[1:])
            return jnp.concatenate([at0, at1], axis=0)

        two = (both_positions(1) * both_positions(2)).astype(BF).astype(F32)
        t = [sf_ref[0, lag:lag + 1, here] for lag in range(3)]
        gate = t[0] * own[8:9] + keeps[2:3, 0:1] * (t[1] * own[7:8]) + keeps[3:4, 0:1] * (t[2] * own[6:7])
        cols = spread([skip_ref[:, here], both_positions(0), keeps[4:5, 0:1] * two[1:] * gate, two])
        taps = taps_ref[8 * b:8 * (b + 1)].astype(BF).astype(F32)
        for g in range(CB // GROUP):
            at = slice(CB * b + GROUP * g, CB * b + GROUP * (g + 1))
            inside = slice(GROUP * g, GROUP * (g + 1))
            c = cols[inside]
            product = prod_ref[at]
            ring = ring_ref[8 * b + g]
            mixed = jnp.dot(jnp.concatenate([halo_ref[b, inside], product], axis=1),
                            jnp.concatenate([ring, ring], axis=0) * masks[...], preferred_element_type=F32)
            skip = lanes_of(c, 0)
            near = ring[:16].astype(F32) * masks[128:144].astype(F32)
            mixed = (mixed + skip * product.astype(F32)
                     + lanes_of(c, 4) * (near[0:1] + jnp.where(lane == 0, skip, 0.0))
                     + lanes_of(c, 5) * (near[1:2] + jnp.where(lane == 1, skip, 0.0)))
            gated = jnp.where(lane == 0, lanes_of(c, 1), jnp.where(lane == 1, lanes_of(c, 2), aux_ref[at])) * mixed
            old = rows_ref[at, 128:].astype(F32)
            after = jnp.where(lane == 0, old + lanes_of(c, 3) * taps[g:g + 1, 127:128], old)
            square = gated * gated
            total0 = total0 + square[:8] + square[8:]
            square = after * after
            total1 = total1 + square[:8] + square[8:]
            out_ref[at, :128] = gated.astype(BF)
            out_ref[at, 128:] = after.astype(BF)
    acc[0], acc[1] = total0, total1

    @pl.when(step == pl.num_programs(0) - 1)
    def _():
        row0 = jnp.sum(acc[0], axis=0, keepdims=True)
        row1 = jnp.sum(acc[1], axis=0, keepdims=True)
        one = lax.broadcasted_iota(jnp.int32, (1, 128), 1)
        sq_ref[...] = jnp.concatenate(
            [row0, jnp.where(one == 0, row1, later_ref[:, :128]), later_ref[:, 128:]], axis=1)


def sf_spec(c):
    return pl.BlockSpec((3, 3, c), lambda i: (0, 0, i))


def tail(docs, base, gate, key, value, sf):
    ch, n = gate.shape
    c = min(BL, ch)
    wide = pl.BlockSpec((c, 256), lambda i: (i, n // 256 - 1))
    return pl.pallas_call(
        tail_kernel, grid=(ch // c,),
        in_specs=[SMEM, SMEM, wide, wide, wide, sf_spec(c)],
        out_specs=pl.BlockSpec((c // CB, ENDS, 128), lambda i: (i, 0, 0)),
        out_shape=jax.ShapeDtypeStruct((ch // CB, ENDS, 128), BF),
        scratch_shapes=[pltpu.VMEM((2, GROUP, 128), BF)],
        compiler_params=pltpu.CompilerParams(vmem_limit_bytes=LATER_VMEM), name="tail",
    )(docs, base, gate, key, value, sf)


def param_specs(c):
    row = pl.BlockSpec((1, c), lambda i: (0, i))
    return [sf_spec(c), row, pl.BlockSpec((c // GROUP, MR), lambda i: (i, 0))]


def later(docs, base, gate, key, value, sf, skip, taps):
    ch, n = gate.shape
    c = min(BL, ch)
    wide = pl.BlockSpec((c, n), lambda i: (i, 0))
    tile = pl.BlockSpec((c, 128), lambda i: (i, 0))
    return pl.pallas_call(
        later_kernel, grid=(ch // c,),
        in_specs=[SMEM, SMEM, wide, wide, wide] + param_specs(c),
        out_specs=[wide, tile, tile, pl.BlockSpec((c // CB, 16, CB), lambda i: (i, 0, 0)),
                   pl.BlockSpec((c // GROUP, MR, MR), lambda i: (i, 0, 0)), pl.BlockSpec((1, n - 128), lambda i: (0, 0))],
        out_shape=[pltpu.HBM((ch, n), BF), jax.ShapeDtypeStruct((ch, 128), F32),
                   jax.ShapeDtypeStruct((ch, 128), BF), jax.ShapeDtypeStruct((ch // CB, 16, CB), BF),
                   jax.ShapeDtypeStruct((ch // GROUP, MR, MR), BF), jax.ShapeDtypeStruct((1, n - 128), F32)],
        scratch_shapes=[pltpu.VMEM((3, 256, 128), BF), pltpu.VMEM((2, GROUP, n), BF), pltpu.VMEM((GROUP, 128), BF),
                        pltpu.VMEM((8, n - 128), F32)],
        cost_estimate=pl.CostEstimate(flops=2 * ch * 384 * 256 * 8, bytes_accessed=8 * ch * n, transcendentals=0),
        compiler_params=pltpu.CompilerParams(vmem_limit_bytes=LATER_VMEM), name="later",
    )(docs, base, gate, key, value, sf, skip, taps)


def first(docs, base, halo, done, sf, skip, taps):
    done = [pltpu.with_memory_space_constraint(x, pltpu.HBM if i == 0 else pltpu.VMEM) for i, x in enumerate(done)]
    rows, aux, prod, own, rings, squares = done
    ch, n = rows.shape
    c = min(BL, ch)
    half = pl.BlockSpec((c, 256), lambda i: (i, 0))
    tile = pl.BlockSpec((c, 128), lambda i: (i, 0))
    whole = lambda w: pl.BlockSpec((1, w), lambda i: (0, 0))
    return pl.pallas_call(
        first_kernel, grid=(ch // c,),
        in_specs=[SMEM, SMEM, pl.BlockSpec((c // CB, ENDS, 128), lambda i: (i, 0, 0)), half, tile, tile,
                  pl.BlockSpec((c // CB, 16, CB), lambda i: (i, 0, 0)),
                  pl.BlockSpec((c // GROUP, MR, MR), lambda i: (i, 0, 0)), whole(n - 128)] + param_specs(c),
        out_specs=[half, whole(n)],
        out_shape=[jax.ShapeDtypeStruct((ch, n), BF), jax.ShapeDtypeStruct((1, n), F32)],
        scratch_shapes=[pltpu.VMEM((256, 128), BF), pltpu.VMEM((8, 128), F32), pltpu.VMEM((2, 8, 128), F32)],
        input_output_aliases={3: 0},
        cost_estimate=pl.CostEstimate(flops=2 * ch * 128 * 256 * 8, bytes_accessed=4 * ch * n, transcendentals=0),
        compiler_params=pltpu.CompilerParams(vmem_limit_bytes=FIRST_VMEM), name="first",
    )(docs, base, halo, rows, aux, prod, own, rings, squares, sf, skip, taps)


FIRST_VMEM = 24 << 20
LATER_VMEM = 40 << 20
def final_kernel(recv_ref, sums_ref, gain_ref, out_ref):
    per, c, n = recv_ref.shape
    gain = jnp.broadcast_to(gain_ref[...], (c, n))
    for i in range(per):
        scale = lax.rsqrt(sums_ref[i] / D + EPS)
        out_ref[:, n * i:n * (i + 1)] = (recv_ref[i].astype(F32) * scale * gain).astype(BF)


def final(recv, sums, gain):
    k, c, n = recv.shape
    per = min(k, PER)
    return pl.pallas_call(
        final_kernel, grid=(k // per,),
        in_specs=[pl.BlockSpec((per, c, n), lambda i: (i, 0, 0)), pl.BlockSpec((per, 1, n), lambda i: (i, 0, 0)),
                  pl.BlockSpec((c, 1), lambda i: (0, 0))],
        out_specs=pl.BlockSpec((c, per * n), lambda i: (0, i)),
        out_shape=jax.ShapeDtypeStruct((c, k * n), BF),
        compiler_params=pltpu.CompilerParams(vmem_limit_bytes=24 << 20), name="settle",
    )(recv, sums, gain)


ROUNDS = (((0, 1), (2, 3), (4, 5), (6, 7)), ((0, 2), (1, 3), (4, 6), (5, 7)), ((0, 7), (1, 6), (2, 5), (3, 4)))


def channel_sum(x):
    if lax.axis_size("ch") != 8:
        return lax.psum(x, "ch"), jnp.zeros_like(x)
    for pairs in ROUNDS[:-1]:
        x = x + lax.ppermute(x, "ch", list(pairs) + [(b, a) for a, b in pairs])
    return x, lax.ppermute(x, "ch", list(ROUNDS[-1]) + [(b, a) for a, b in ROUNDS[-1]])


def local(gate, key, value, sf, taps, skip, gain, docs):
    place = lax.axis_index("ctx")
    width = lax.axis_size("ctx")
    ch, n = gate.shape
    base = (place * n).astype(jnp.int32).reshape(1)
    skip = skip.reshape(1, ch)
    gain = lax.dynamic_slice_in_dim(gain, place * (ch // width), ch // width).reshape(ch // width, 1)
    gate, key, value = (pltpu.with_memory_space_constraint(x, pltpu.HBM) for x in (gate, key, value))
    ends = tail(pltpu.with_memory_space_constraint(docs, pltpu.HBM), base, gate, key, value, pltpu.with_memory_space_constraint(sf, pltpu.HBM))
    halo = lax.ppermute(ends, "ctx", [(i, i + 1) for i in range(width - 1)])
    done = later(docs, base, gate, key, value, sf, skip, taps)
    rows, squares = first(docs, base, halo, done, sf, skip, taps)
    recv = lax.all_to_all(rows.reshape(width, ch // width, n), "ctx", split_axis=0, concat_axis=0, tiled=True)
    near, far = channel_sum(squares)
    far, recv = lax.optimization_barrier((far, recv))
    sums = lax.all_to_all(jnp.broadcast_to((near + far)[None], (width, 1, n)), "ctx", split_axis=0, concat_axis=0, tiled=True)
    return final(recv, sums, gain)


def solution(mesh):
    in_specs = (P("ch", "ctx"),) * 3 + (P(None, None, "ch"), P("ch", None), P("ch"), P("ch"), P())
    return jax.shard_map(local, mesh=mesh, in_specs=in_specs, out_specs=P(("ch", "ctx"), None), check_vma=False)
```
